256 devices in a mesh: ctx: 8 (over x, core), exp: 32 (over y, z).
Axes of the slice: x: 4, y: 4, z: 8, core: 2. Of those that a mesh axis runs over, the one named last changes fastest.
Arguments:
- queries: bfloat16 [32, 1024, 1024], P('exp', 'ctx'), may hold values from -6 to 6
- keys: bfloat16 [32, 1024, 1024], P('exp', 'ctx'), may hold values from -6 to 6
- values: bfloat16 [32, 1024, 2048], P('exp', 'ctx'), may hold values from -6 to 6
- out_gate: bfloat16 [32, 1024, 2048], P('exp', 'ctx'), may hold values from -6 to 6
- write_rate: float32 [32, 1024, 16], P('exp', 'ctx'), may hold values from 0.02 to 0.2
- decay: float32 [32, 1024, 16], P('exp', 'ctx'), may hold values from 0.6 to 1
- head_gain: float32 [128], replicated, may hold values from 0.1 to 1.9
- residual: bfloat16 [32, 1024, 2048], P('exp', 'ctx'), may hold values from -6 to 6
- out_proj: bfloat16 [2048, 2048], P('ctx'), may hold values from -0.125 to 0.125
- ffn_gain: float32 [2048], replicated, may hold values from 0.25 to 1.75
- expert_ids: int32 [32, 1024, 10], P('exp', 'ctx'), may hold values from 0 to 511, all different within a row; in each aligned block of 128 rows (0 to 127, 128 to 255, ..., all dimensions but the last counted through in order) at most 4 rows name the same one
- route_weight: float32 [32, 1024, 10], P('exp', 'ctx'), may hold values from 0.1 to 0.4
- w_gate: bfloat16 [256, 2048, 512], P(('ctx', 'exp')), may hold values from -0.125 to 0.125
- w_up: bfloat16 [256, 2048, 512], P(('ctx', 'exp')), may hold values from -0.125 to 0.125
- w_down: bfloat16 [256, 512, 2048], P(('ctx', 'exp')), may hold values from -0.25 to 0.25
- ablate_mask: int32 [32, 1024], P('exp', 'ctx'), may hold values 0 or 1
- direction: float32 [2048], replicated, may hold values from -6 to 6
Outputs:
- layer_out: bfloat16 [32, 1024, 2048], P('exp', 'ctx')
The draws below stay inside these ranges and needn't reach their ends.
Inputs may be any that keep to these rules, and one draw needn't show every extreme that they name: `expert_ids`: A token's 10 experts differ; within the rows of one device (aligned blocks of 128 tokens of a sequence) no expert is named more than 4 times.
All inputs are finite; a program needn't handle non-finite values. No bound on the sum of `ablate_mask` on one device may be relied on, other than what follows from the above.
Results may differ from the reference program's by a relative error of at most 0.0044.
Values may be sent and summed in bfloat16 or wider, within the bound.
A program may use at most 128 MiB of HBM per device.

```python
import math
import jax
import jax.numpy as jnp
import numpy as np
from jax import lax

D = 2048
CONTENT_MIXERS = 16
KH = 8
DK = 128
DV = 128
FE = 512
ROUTED = 512
TOP = 10
SHARD_POSITIONS = 128
CAP = 4
EXPERTS = 256
PROMPT_GROUP = 32
SPAN_POSITIONS = 1024
N_CTX = 8


def draw_decay(key, part):
    stochastic_seed_parts = jax.random.split(key, 7)
    segment_number = SPAN_POSITIONS // SHARD_POSITIONS
    fast_share = 0.5
    fast_heads = jax.random.uniform(stochastic_seed_parts[0], (PROMPT_GROUP, 1, 1, CONTENT_MIXERS)) < fast_share
    fast_rate = jax.random.uniform(stochastic_seed_parts[1], (PROMPT_GROUP, 1, 1, CONTENT_MIXERS), minval=1.0 / 50.0, maxval=1.0 / 30.0)
    slow_rate = jax.random.uniform(stochastic_seed_parts[2], (PROMPT_GROUP, 1, 1, CONTENT_MIXERS), minval=0.02, maxval=0.2) * (math.log(10.0) / SPAN_POSITIONS)
    reference_frequency = jnp.where(fast_heads, fast_rate, slow_rate)
    segment_multiplier = jnp.exp(jax.random.uniform(stochastic_seed_parts[3], (PROMPT_GROUP, segment_number, 1, CONTENT_MIXERS), minval=math.log(0.6), maxval=math.log(1.6)))
    unevenness_level = jax.random.uniform(stochastic_seed_parts[4], (PROMPT_GROUP, segment_number, SHARD_POSITIONS, CONTENT_MIXERS), minval=0.5, maxval=1.5)
    cluster_occurrences = jax.random.uniform(stochastic_seed_parts[5], (PROMPT_GROUP, segment_number, SHARD_POSITIONS, 1)) < 2.0 / SPAN_POSITIONS
    cluster_surviving = jnp.where(cluster_occurrences, jax.random.uniform(stochastic_seed_parts[6], (PROMPT_GROUP, segment_number, SHARD_POSITIONS, CONTENT_MIXERS), minval=0.7, maxval=0.8), 1.0)
    content_outcomes = jnp.exp(-reference_frequency * segment_multiplier * unevenness_level) * cluster_surviving
    return content_outcomes.reshape(PROMPT_GROUP, SPAN_POSITIONS, CONTENT_MIXERS).astype(jnp.float32)


def with_ends(values, key, low, top_value):
    extent = values.shape
    spot = [jax.random.randint(jax.random.fold_in(key, axis), (), 0, extent[axis]) for axis in range(len(extent))]
    values = values.at[tuple(spot)].set(low)
    longest = extent.index(max(extent))
    spot[longest] = (spot[longest] + 1) % extent[longest]
    return values.at[tuple(spot)].set(top_value)


def shard_levels(own_key, shape, pieces, low, high):
    factor_of = 1.0
    for position, shards_of in pieces:
        heights = jax.random.uniform(jax.random.fold_in(jax.random.fold_in(own_key, 6), position), (shards_of,), jnp.float32, low / len(pieces), high / len(pieces))
        factor_of = factor_of * jnp.repeat(jnp.exp(heights), shape[position] // shards_of).reshape((-1,) + (1,) * (len(shape) - 1 - position))
    return factor_of


def routed_block(key, own, number, rows, amount, top, bound, skew):
    sequence = jax.random.permutation(key, amount)
    crowded, ordinary = load_shares(amount, rows * top, bound, skew, True), load_shares(amount, rows * top, bound, skew, False)
    places = jnp.arange(amount)

    def named(lengths, offset_by):
        used = int((lengths > 0).sum())
        fixed = max(1, used // 4)
        shifted = fixed + (places - fixed + offset_by * (used - fixed)) % max(1, amount - fixed)
        return jnp.zeros((amount,), jnp.int32).at[sequence[jnp.where(places < fixed, places, shifted)]].set(jnp.asarray(lengths, jnp.int32))

    lengths = jnp.where(number % 4 == 0, named(crowded, number // 4), named(ordinary, number - number // 4 - 1))
    mixed = jax.random.permutation(jax.random.fold_in(own, 3), amount)
    source_of, receiver = mixed[0:amount // 2 * 2:2], mixed[1:amount // 2 * 2:2]
    room = jnp.minimum(lengths[source_of] - 1, bound - lengths[receiver]) // 2
    room = jnp.where((source_of == sequence[0]) | (receiver == sequence[0]) | (lengths[receiver] == 0), 0, jnp.maximum(room, 0))
    shifted = jax.random.randint(jax.random.fold_in(own, 4), (amount // 2,), 0, 1 << 20) % (room + 1)
    lengths = lengths.at[source_of].add(-shifted).at[receiver].add(shifted)
    labels = jnp.searchsorted(jnp.cumsum(lengths), jnp.arange(rows * top), side="right").astype(jnp.int32)
    listing = labels.reshape(top, rows).T
    listing = listing[jax.random.permutation(jax.random.fold_in(own, 1), rows)]
    offset_by = jax.random.randint(jax.random.fold_in(own, 2), (rows, 1), 0, top)
    return jnp.take_along_axis(listing, (jnp.arange(top)[None, :] + offset_by) % top, axis=1)


def load_shares(count, total, bound, lean, full):
    portions = [(1 << 20) // math.isqrt(rank ** lean) + 1 for rank in range(1, count + 1)]
    largest = bound if full else min(bound, max(-(-total // count), total * portions[0] // sum(portions)))
    least = 1 if total - largest >= count - 1 else 0
    holding, surplus = [largest] + [least] * (count - 1), total - largest - least * (count - 1)
    while surplus > 0:
        free = [i for i in range(1, count) if holding[i] < largest] or [i for i in range(1, count) if holding[i] < bound]
        whole, left = sum([portions[i] for i in free]), surplus
        for i in free:
            extra = min(bound - holding[i], max(1, left * portions[i] // whole), surplus)
            holding[i] = holding[i] + extra
            surplus = surplus - extra
    return np.array(holding)


def scatter_about(key, extent, width, limit, pieces=(), kind=jnp.bfloat16):
    loudness = shard_levels(key, extent, pieces, -0.22, 0.18) if pieces else 1.0
    values = jax.random.normal(key, extent, jnp.float32) * width * loudness
    return jnp.minimum(jnp.maximum(values, -limit), limit).astype(kind)


def setup_inputs(seed: int = 0) -> dict:
    splits = jax.random.split(jax.random.key(seed), 18)
    queries = scatter_about(splits[0], (PROMPT_GROUP, SPAN_POSITIONS, KH * DK), 1.0, 6.0, ((0, 32), (1, 8)))
    keys = scatter_about(splits[1], (PROMPT_GROUP, SPAN_POSITIONS, KH * DK), 1.0, 6.0, ((0, 32), (1, 8)))
    values = scatter_about(splits[2], (PROMPT_GROUP, SPAN_POSITIONS, CONTENT_MIXERS * DV), 1.0, 6.0, ((0, 32), (1, 8)))
    out_gate = scatter_about(splits[3], (PROMPT_GROUP, SPAN_POSITIONS, CONTENT_MIXERS * DV), 1.0, 6.0, ((0, 32), (1, 8)))
    write_rate = jnp.clip(0.02 + 0.18 * jax.random.uniform(splits[4], (PROMPT_GROUP, SPAN_POSITIONS, CONTENT_MIXERS), jnp.float32) ** shard_levels(splits[4], (PROMPT_GROUP, SPAN_POSITIONS, CONTENT_MIXERS), ((0, 32), (1, 8)), -0.2, 0.2), 0.02, 0.2)
    decay = draw_decay(jax.random.fold_in(splits[17], 71), 0)
    head_gain = jnp.clip(1.0 + 0.18 * jax.random.normal(splits[6], (DV,), jnp.float32), 0.1, 1.9)
    residual = scatter_about(splits[7], (PROMPT_GROUP, SPAN_POSITIONS, D), 1.0, 6.0, ((0, 32), (1, 8)))
    out_proj = scatter_about(splits[8], (CONTENT_MIXERS * DV, D), (CONTENT_MIXERS * DV) ** -0.5, 0.125, ((0, 8),))
    ffn_gain = jnp.clip(1.0 + 0.15 * jax.random.normal(splits[9], (D,), jnp.float32), 0.25, 1.75)
    expert_ids_keys = jax.random.split(jax.random.fold_in(splits[10], 1), PROMPT_GROUP * SPAN_POSITIONS // SHARD_POSITIONS)
    expert_ids_turns = jax.random.permutation(jax.random.fold_in(splits[10], 3), PROMPT_GROUP * SPAN_POSITIONS // SHARD_POSITIONS)
    expert_ids = jax.vmap(lambda own, number: routed_block(jax.random.fold_in(splits[10], 2), own, number, SHARD_POSITIONS, ROUTED, TOP, CAP, 1))(expert_ids_keys, expert_ids_turns).reshape((PROMPT_GROUP, SPAN_POSITIONS, TOP))
    route_weight = jnp.clip(0.1 + 0.3 * jax.random.uniform(splits[11], (PROMPT_GROUP, SPAN_POSITIONS, TOP), jnp.float32) ** shard_levels(splits[11], (PROMPT_GROUP, SPAN_POSITIONS, TOP), ((0, 32), (1, 8)), -0.2, 0.2), 0.1, 0.4)
    w_gate = scatter_about(splits[12], (EXPERTS, D, FE), D ** -0.5, 0.125, ((0, 256),))
    w_up = scatter_about(splits[13], (EXPERTS, D, FE), D ** -0.5, 0.125, ((0, 256),))
    w_down = scatter_about(splits[14], (EXPERTS, FE, D), FE ** -0.5, 0.25, ((0, 256),))
    ablate_mask = with_ends((jax.random.randint(splits[15], (PROMPT_GROUP, SPAN_POSITIONS), 0, 2) < 1).astype(jnp.int32), jax.random.fold_in(splits[15], 1), 0, 1)
    direction = scatter_about(splits[16], (D,), 1.0, 6.0, (), jnp.float32)
    return dict(queries=queries, keys=keys, values=values, out_gate=out_gate, write_rate=write_rate, decay=decay, head_gain=head_gain, residual=residual, out_proj=out_proj, ffn_gain=ffn_gain, expert_ids=expert_ids, route_weight=route_weight, w_gate=w_gate, w_up=w_up, w_down=w_down, ablate_mask=ablate_mask, direction=direction)


HIGHEST = lax.Precision.HIGHEST

def block_maps(query_f, key_unit, value_f, write_f, decay_f):
    length_b = decay_f.shape[-1]
    width_k = key_unit.shape[-1]
    log_decay = jnp.cumsum(jnp.log(decay_f), axis=-1)
    row_ids = lax.broadcasted_iota(jnp.int32, (length_b, length_b), 0)
    col_ids = lax.broadcasted_iota(jnp.int32, (length_b, length_b), 1)
    on_after = (row_ids >= col_ids).astype(jnp.float32)
    strictly = (row_ids > col_ids).astype(jnp.float32)
    ratios = jnp.exp(jnp.minimum(log_decay[..., :, None] - log_decay[..., None, :], 0.0)) * on_after
    cumulative = jnp.exp(log_decay)
    key_dots = jnp.einsum('...id,...jd->...ij', key_unit, key_unit, precision=HIGHEST)
    system = jnp.eye(length_b, dtype=jnp.float32) + write_f[..., :, None] * ratios * strictly * key_dots
    writes = jax.scipy.linalg.solve_triangular(system, write_f[..., None] * value_f, lower=True, unit_diagonal=True)
    erases = jax.scipy.linalg.solve_triangular(system, (write_f * cumulative)[..., None] * key_unit, lower=True, unit_diagonal=True)
    scores = jnp.einsum('...id,...jd->...ij', query_f, key_unit, precision=HIGHEST) * ratios
    local_out = jnp.einsum('...ij,...jv->...iv', scores, writes, precision=HIGHEST)
    query_eff = cumulative[..., None] * query_f - jnp.einsum('...ij,...jd->...id', scores, erases, precision=HIGHEST)
    remaining = jnp.exp(log_decay[..., -1:] - log_decay)
    weighted = remaining[..., None] * key_unit
    carried = jnp.einsum('...jd,...je->...de', weighted, erases, precision=HIGHEST)
    transition = cumulative[..., -1][..., None, None] * jnp.eye(width_k, dtype=jnp.float32) - carried
    offset = jnp.einsum('...jd,...jv->...dv', weighted, writes, precision=HIGHEST)
    return (local_out, query_eff, transition, offset)

def blocks_of_heads(array):
    shaped = array.reshape(PROMPT_GROUP, N_CTX, SHARD_POSITIONS, CONTENT_MIXERS, array.shape[-1])
    return shaped.transpose(1, 0, 3, 2, 4)

def blocks_of_rates(array):
    shaped = array.reshape(PROMPT_GROUP, N_CTX, SHARD_POSITIONS, CONTENT_MIXERS)
    return shaped.transpose(1, 0, 3, 2)

def reference(queries, keys, values, out_gate, write_rate, decay, head_gain, residual, out_proj, ffn_gain, expert_ids, route_weight, w_gate, w_up, w_down, ablate_mask, direction):
    group_size = CONTENT_MIXERS // KH
    query_raw = jnp.repeat(queries.astype(jnp.float32).reshape(PROMPT_GROUP, SPAN_POSITIONS, KH, DK), group_size, axis=2)
    query_f = query_raw / jnp.sqrt(lax.optimization_barrier(jnp.sum(query_raw * query_raw, -1, keepdims=True)) + 1e-06) * DK ** (-0.5)
    key_f = jnp.repeat(keys.astype(jnp.float32).reshape(PROMPT_GROUP, SPAN_POSITIONS, KH, DK), group_size, axis=2)
    key_unit = key_f / jnp.sqrt(lax.optimization_barrier(jnp.sum(key_f * key_f, -1, keepdims=True)) + 1e-06)
    value_f = values.astype(jnp.float32).reshape(PROMPT_GROUP, SPAN_POSITIONS, CONTENT_MIXERS, DV)

    def advance(state, inputs):
        query_b, key_b, value_b, write_b, decay_b = inputs
        local_out, query_eff, transition, offset = block_maps(query_b, key_b, value_b, write_b, decay_b)
        block_out = local_out + jnp.einsum('bhid,bhdv->bhiv', query_eff, state, precision=HIGHEST)
        next_state = jnp.einsum('bhij,bhjv->bhiv', transition, state, precision=HIGHEST) + offset
        return (next_state, block_out)
    start_state = jnp.zeros((PROMPT_GROUP, CONTENT_MIXERS, DK, DV), jnp.float32)
    _, block_outs = lax.scan(advance, start_state, (blocks_of_heads(query_f), blocks_of_heads(key_unit), blocks_of_heads(value_f), blocks_of_rates(write_rate), blocks_of_rates(decay)))
    head_out = block_outs.transpose(1, 0, 3, 2, 4).reshape(PROMPT_GROUP, SPAN_POSITIONS, CONTENT_MIXERS, DV)
    mean_square = lax.optimization_barrier(jnp.mean(head_out * head_out, -1, keepdims=True))
    gate_f = out_gate.astype(jnp.float32).reshape(PROMPT_GROUP, SPAN_POSITIONS, CONTENT_MIXERS, DV)
    normed = head_out / jnp.sqrt(mean_square + 1e-06) * head_gain * jax.nn.silu(gate_f)
    tokens_all = PROMPT_GROUP * SPAN_POSITIONS
    mixed = normed.reshape(tokens_all, CONTENT_MIXERS * DV).astype(jnp.bfloat16)
    projected = jnp.dot(mixed.astype(jnp.float32), out_proj.astype(jnp.float32), preferred_element_type=jnp.float32)
    hidden_sum = residual.reshape(tokens_all, D).astype(jnp.float32) + projected
    ffn_in = (hidden_sum / jnp.sqrt(lax.optimization_barrier(jnp.mean(hidden_sum * hidden_sum, -1, keepdims=True)) + 1e-06) * ffn_gain).astype(jnp.bfloat16)
    blocks = tokens_all // SHARD_POSITIONS
    block_ids_list = expert_ids.reshape(blocks, SHARD_POSITIONS * TOP)
    expert_range = jnp.arange(EXPERTS, dtype=jnp.int32)

    def slot_of(row_list):
        one_hot = (row_list[:, None] == expert_range[None, :]).astype(jnp.int32)
        return lax.optimization_barrier(jnp.sum(jnp.cumsum(one_hot, axis=0) * one_hot, axis=1)) - 1
    slots = lax.map(slot_of, block_ids_list)
    in_window = block_ids_list < EXPERTS
    block_ids = jnp.arange(blocks, dtype=jnp.int32)[:, None]
    token_index = block_ids * SHARD_POSITIONS + jnp.arange(SHARD_POSITIONS * TOP, dtype=jnp.int32)[None, :] // TOP
    row_pick = jnp.where(in_window, block_ids_list, EXPERTS)
    col_pick = jnp.where(in_window, block_ids * CAP + slots, 0)
    index_table = jnp.full((EXPERTS + 1, blocks * CAP), tokens_all, jnp.int32).at[row_pick, col_pick].set(token_index)[:EXPERTS]
    weight_table = jnp.zeros((EXPERTS + 1, blocks * CAP), jnp.float32).at[row_pick, col_pick].set(route_weight.reshape(blocks, SHARD_POSITIONS * TOP))[:EXPERTS]
    padded_in = jnp.concatenate([ffn_in, jnp.zeros((1, D), jnp.bfloat16)], axis=0)

    def expert_step(running, inputs):
        index_row, weight_row, gate_mat, up_mat, down_mat = inputs
        rows_in = padded_in[index_row]
        gate_part = jnp.dot(rows_in.astype(jnp.float32), gate_mat.astype(jnp.float32), preferred_element_type=jnp.float32)
        up_part = jnp.dot(rows_in.astype(jnp.float32), up_mat.astype(jnp.float32), preferred_element_type=jnp.float32)
        activated = (jax.nn.silu(gate_part) * up_part).astype(jnp.bfloat16)
        expert_out = jnp.dot(activated.astype(jnp.float32), down_mat.astype(jnp.float32), preferred_element_type=jnp.float32).astype(jnp.bfloat16)
        running = running.at[index_row].add(weight_row[:, None] * expert_out.astype(jnp.float32))
        return (running, None)
    moe_start = jnp.zeros((tokens_all + 1, D), jnp.float32)
    moe_total, _ = lax.scan(expert_step, moe_start, (index_table, weight_table, w_gate, w_up, w_down))
    combined = hidden_sum + moe_total[:tokens_all]
    unit_dir = direction / jnp.sqrt(jnp.sum(direction * direction) + 1e-06)
    along = jnp.dot(combined, unit_dir, precision=HIGHEST)
    mask_f = ablate_mask.reshape(tokens_all).astype(jnp.float32)
    layer_out = combined - (mask_f * along)[:, None] * unit_dir[None, :]
    return layer_out.astype(jnp.bfloat16).reshape(PROMPT_GROUP, SPAN_POSITIONS, D)
```

```python
import jax
import jax.numpy as jnp
from jax import lax
from jax.experimental import pallas as pl
from jax.experimental.pallas import tpu as pltpu
from jax.sharding import PartitionSpec as P

D = 2048
HEADS = 16
KH = 8
DK = 128
DV = 128
T = 128
TOP = 10
CAP = 4
N_CTX = 8
STATE = jnp.float32
F32 = jnp.float32
BF16 = jnp.bfloat16
HIGHEST = lax.Precision.HIGHEST
MESH = pl.DeviceIdType.MESH


def split(a, parts):
    if a.dtype == BF16:
        return [a]
    pieces = []
    for _ in range(parts):
        piece = a.astype(BF16)
        pieces.append(piece)
        a = a - piece.astype(F32)
    return pieces


def mm(a, b, na=1, nb=1):
    total = None
    for i, x in enumerate(split(a, na)):
        for j, y in enumerate(split(b, nb)):
            if i + j < max(na, nb):
                term = jnp.dot(x, y, preferred_element_type=F32)
                total = term if total is None else total + term
    return total


def mm_t(a, b):
    return lax.dot_general(a, b, (((1,), (1,)), ((), ())), preferred_element_type=F32)


def mixer_kernel(
    q_ref, k_ref, v_ref, gate_ref, w_ref, wt_ref, d_ref, dt_ref, gain_ref, out_ref,
    lc_ref, lr_ref, loc_ref, qeff_ref, car_ref, off_ref, got_ref, sent_ref, send_sem, recv_sem,
):
    me = lax.axis_index("ctx")
    last = N_CTX - 1
    barrier = pltpu.get_barrier_semaphore()

    @pl.when(me > 0)
    def _():
        pl.semaphore_signal(barrier, inc=1, device_id={"ctx": me - 1}, device_id_type=MESH)

    @pl.when(me < last)
    def _():
        pl.semaphore_signal(barrier, inc=1, device_id={"ctx": me + 1}, device_id_type=MESH)

    rows = lax.broadcasted_iota(jnp.int32, (T, T), 0)
    cols = lax.broadcasted_iota(jnp.int32, (T, T), 1)
    lower = (rows >= cols).astype(F32)
    upper = (rows <= cols).astype(F32)
    eye = (rows == cols).astype(F32)
    lc_ref[...] = jnp.dot(lower, jnp.log(d_ref[...]), precision=HIGHEST, preferred_element_type=F32)
    lr_ref[...] = jnp.dot(jnp.log(dt_ref[...]), upper, precision=HIGHEST, preferred_element_type=F32)
    ones = jnp.ones((8, DK), F32)
    head_lane = lax.broadcasted_iota(jnp.int32, (T, HEADS), 1)
    in_16 = (rows // 16 == cols // 16) & (rows > cols)

    def column(array, h):
        return jnp.sum(jnp.where(head_lane == h, array, 0.0), axis=1, keepdims=True)

    def maps(step, carry):
        groups = [step * 2, step * 2 + 1]
        per_group = []
        for g in groups:
            at = pl.ds(pl.multiple_of(g * DK, DK), DK)
            kraw, qraw = k_ref[:, at], q_ref[:, at]
            kf, qf = kraw.astype(F32), qraw.astype(F32)
            ksq = kf * kf
            rk = lax.rsqrt(jnp.sum(ksq, axis=1, keepdims=True) + 1e-06)
            rk_row = lax.rsqrt(
                lax.dot_general(
                    ones, ksq, (((1,), (1,)), ((), ())), precision=HIGHEST, preferred_element_type=F32
                )[0:1] + 1e-06
            )
            rq = lax.rsqrt(jnp.sum(qf * qf, axis=1, keepdims=True) + 1e-06) * DK ** (-0.5)
            kk = mm_t(kraw, kraw) * rk * rk_row
            qk = mm_t(qraw, kraw) * rq * rk_row
            kt = kf.T * rk_row
            per_group.append((kraw, qf * rq, rk_row, kk, qk, kt))
        heads = []
        for i, g in enumerate(groups):
            for j in range(2):
                heads.append((per_group[i], g * 2 + j))
        state = []
        for (kraw, qu, rk_row, kk, qk, kt), h in heads:
            lcol = column(lc_ref[...], h)
            wcol = column(w_ref[...], h)
            lrow = lr_ref[pl.ds(h, 1), :]
            wrow = wt_ref[pl.ds(h, 1), :]
            ratio = jnp.exp(jnp.minimum(lcol - lrow, 0.0)) * lower
            a = jnp.where(rows > cols, ratio * kk, 0.0) * wcol
            remain = jnp.exp(lrow[:, T - 1 : T] - lrow)
            g2 = jnp.concatenate([qk * ratio, kt * remain], axis=0)
            state.append((a, g2, wrow, wrow * jnp.exp(lrow) * rk_row, jnp.exp(lcol)))
        n = range(len(heads))
        a = [s[0] for s in state]
        dg = [jnp.where(in_16, x, 0.0) for x in a]
        d2 = [mm(x, x) for x in dg]
        d3 = [mm(dg[i], d2[i]) for i in n]
        d4 = [mm(x, x) for x in d2]
        m1 = [eye - dg[i] + d2[i] - d3[i] for i in n]
        d8 = [mm(x, x) for x in d4]
        m2 = [m1[i] + mm(m1[i], d4[i]) for i in n]
        inv = [m2[i] + mm(m2[i], d8[i]) for i in n]
        for size in (16, 32, 64):
            band = (rows // (2 * size) == cols // (2 * size)) & (rows // size > cols // size)
            part = [jnp.where(band, x, 0.0) for x in a]
            half = [mm(part[i], inv[i]) for i in n]
            inv = [inv[i] - mm(inv[i], half[i]) for i in n]
        y = [mm(state[i][1], inv[i], 2, 2) for i in n]
        for i in n:
            (kraw, qu, rk_row, kk, qk, kt), h = heads[i]
            _, _, w1, w2, cum = state[i]
            vraw = v_ref[:, pl.ds(pl.multiple_of(h * DV, DV), DV)]
            z1 = mm(y[i] * w1, vraw, 2)
            z2 = mm(y[i] * w2, kraw, 2)
            loc_ref[h] = z1[:T]
            off_ref[h] = z1[T:]
            qeff_ref[h] = cum * qu - z2[:T]
            car_ref[h] = z2[T:]
        return carry

    lax.fori_loop(0, KH // 2, maps, 0)

    @pl.when((me > 0) & (me < last))
    def _():
        pl.semaphore_wait(barrier, 2)

    @pl.when((me == 0) | (me == last))
    def _():
        pl.semaphore_wait(barrier, 1)

    def hop(h):
        return pltpu.make_async_remote_copy(
            src_ref=sent_ref.at[h],
            dst_ref=got_ref.at[h],
            send_sem=send_sem.at[h],
            recv_sem=recv_sem.at[h],
            device_id={"ctx": jnp.minimum(me + 1, last)},
            device_id_type=MESH,
        )

    def fraction(h):
        return jnp.exp(lr_ref[pl.ds(h, 1), T - 1 : T])

    @pl.when(me == 0)
    def _():
        def start(h, carry):
            got_ref[h] = jnp.zeros((DK, DV), STATE)
            sent_ref[h] = off_ref[h].astype(STATE)
            hop(h).start()
            return carry

        lax.fori_loop(0, HEADS, start, 0)

    @pl.when((me > 0) & (me < last))
    def _():
        def relay(h, carry):
            hop(h).wait_recv()
            s = got_ref[h].astype(F32)
            sent_ref[h] = (fraction(h) * s + off_ref[h] - mm(car_ref[h], s, 2, 2)).astype(STATE)
            hop(h).start()
            return carry

        lax.fori_loop(0, HEADS, relay, 0)

    gain = gain_ref[...]

    def finish(h, carry):
        @pl.when(me == last)
        def _():
            hop(h).wait_recv()

        o = loc_ref[h] + mm(qeff_ref[h], got_ref[h].astype(F32), 2, 2)
        at = pl.ds(pl.multiple_of(h * DV, DV), DV)
        gate = gate_ref[:, at].astype(F32)
        scale = lax.rsqrt(jnp.mean(o * o, axis=1, keepdims=True) + 1e-06)
        out_ref[:, at] = (o * scale * gain * (gate / (1.0 + jnp.exp(-gate)))).astype(BF16)
        return carry

    lax.fori_loop(0, HEADS, finish, 0)

    @pl.when(me < last)
    def _():
        def drain(h, carry):
            hop(h).wait_send()
            return carry

        lax.fori_loop(0, HEADS, drain, 0)


def mixer(queries, keys, values, out_gate, write_rate, decay, head_gain):
    square = pltpu.VMEM((HEADS, DK, DV), F32)
    return pl.pallas_call(
        mixer_kernel,
        out_shape=jax.ShapeDtypeStruct((T, HEADS * DV), BF16),
        in_specs=[pl.BlockSpec(memory_space=pltpu.VMEM)] * 9,
        out_specs=pl.BlockSpec(memory_space=pltpu.VMEM),
        scratch_shapes=[
            pltpu.VMEM((T, HEADS), F32),
            pltpu.VMEM((HEADS, T), F32),
            square, square, square, square,
            pltpu.VMEM((HEADS, DK, DV), STATE),
            pltpu.VMEM((HEADS, DK, DV), STATE),
            pltpu.SemaphoreType.DMA((HEADS,)),
            pltpu.SemaphoreType.DMA((HEADS,)),
        ],
        compiler_params=pltpu.CompilerParams(
            collective_id=0, has_side_effects=True, vmem_limit_bytes=40 * 2**20
        ),
        cost_estimate=pl.CostEstimate(flops=20 * 10**9, bytes_accessed=2 * 10**6, transcendentals=0),
        name="mixer",
    )(queries, keys, values, out_gate, write_rate, write_rate.T, decay, decay.T, head_gain[None, :])


def local(
    queries, keys, values, out_gate, write_rate, decay, head_gain, residual, out_proj, ffn_gain,
    expert_ids, route_weight, w_gate, w_up, w_down, ablate_mask, direction,
):
    mixed = mixer(queries[0], keys[0], values[0], out_gate[0], write_rate[0], decay[0], head_gain)
    projected = jnp.dot(
        mixed, lax.all_gather(out_proj, "ctx", axis=0, tiled=True), preferred_element_type=F32
    )
    hidden_sum = residual[0].astype(F32) + projected
    ffn_in = (
        hidden_sum / jnp.sqrt(jnp.mean(hidden_sum * hidden_sum, -1, keepdims=True) + 1e-06) * ffn_gain
    ).astype(BF16)
    n_ctx, n_exp = lax.axis_size("ctx"), lax.axis_size("exp")
    window = n_ctx * n_exp
    ids = expert_ids[0]
    named = ids[:, :, None] == jnp.arange(window, dtype=jnp.int32)[None, None, :]
    member = jnp.sum(named.astype(F32), axis=1)
    weight = jnp.sum(jnp.where(named, route_weight[0][:, :, None], 0.0), axis=1)
    earlier = jnp.tril(jnp.ones((T, T), F32), -1)
    slot = jnp.dot(earlier, member, preferred_element_type=F32)
    slots = jnp.arange(CAP, dtype=F32)
    taken = (slot[:, :, None] == slots) & (member[:, :, None] > 0)
    pick = taken.astype(BF16).reshape(T, window * CAP)
    weights = jnp.where(taken, weight[:, :, None], 0.0).reshape(T, window * CAP)
    outgoing = jnp.dot(pick.T, ffn_in, preferred_element_type=F32).astype(BF16)
    outgoing = outgoing.reshape(n_ctx, n_exp, CAP, D)

    def exchange(rows):
        rows = lax.all_to_all(rows, "exp", split_axis=1, concat_axis=1, tiled=True)
        return lax.all_to_all(rows, "ctx", split_axis=0, concat_axis=0, tiled=True)

    rows = exchange(outgoing).reshape(-1, D)
    gate_part = jnp.dot(rows, w_gate[0], preferred_element_type=F32)
    up_part = jnp.dot(rows, w_up[0], preferred_element_type=F32)
    act = (jax.nn.silu(gate_part) * up_part).astype(BF16)
    expert_out = jnp.dot(act, w_down[0], preferred_element_type=F32).astype(BF16)
    returned = exchange(expert_out.reshape(n_ctx, n_exp, CAP, D)).reshape(-1, D)
    high = weights.astype(BF16)
    rest = (weights - high.astype(F32)).astype(BF16)
    moe_sum = jnp.dot(high, returned, preferred_element_type=F32) + jnp.dot(
        rest, returned, preferred_element_type=F32
    )
    combined = hidden_sum + moe_sum
    unit_dir = direction / jnp.sqrt(jnp.sum(direction * direction) + 1e-06)
    along = jnp.sum(combined * unit_dir[None, :], axis=1)
    mask_f = ablate_mask[0].astype(F32)
    layer_out = combined - (mask_f * along)[:, None] * unit_dir[None, :]
    return layer_out.astype(BF16)[None]


def solution(mesh):
    tokens = P("exp", "ctx", None)
    experts = P(("ctx", "exp"), None, None)
    placed = (
        tokens, tokens, tokens, tokens, tokens, tokens, P(), tokens, P("ctx", None), P(),
        tokens, tokens, experts, experts, experts, P("exp", "ctx"), P(),
    )
    return jax.shard_map(local, mesh=mesh, in_specs=placed, out_specs=tokens, check_vma=False)
```

```python
import jax
import jax.numpy as jnp
from jax import lax
from jax.experimental import pallas as pl
from jax.experimental.pallas import tpu as pltpu
from jax.sharding import PartitionSpec as P

D = 2048
HEADS = 16
KH = 8
DK = 128
DV = 128
T = 128
TOP = 10
CAP = 4
N_CTX = 8
STATE = jnp.float32
F32 = jnp.float32
BF16 = jnp.bfloat16
HIGHEST = lax.Precision.HIGHEST
MESH = pl.DeviceIdType.MESH


def split(a, parts):
    if a.dtype == BF16:
        return [a]
    pieces = []
    for _ in range(parts):
        piece = a.astype(BF16)
        pieces.append(piece)
        a = a - piece.astype(F32)
    return pieces


def mm(a, b, na=1, nb=1):
    total = None
    for i, x in enumerate(split(a, na)):
        for j, y in enumerate(split(b, nb)):
            if i + j < max(na, nb):
                term = jnp.dot(x, y, preferred_element_type=F32)
                total = term if total is None else total + term
    return total


def mm_t(a, b):
    return lax.dot_general(a, b, (((1,), (1,)), ((), ())), preferred_element_type=F32)


def mixer_kernel(
    q_ref, k_ref, v_ref, gate_ref, w_ref, wt_ref, d_ref, dt_ref, gain_ref, out_ref,
    lc_ref, lr_ref, loc_ref, qeff_ref, car_ref, off_ref, got_ref, sent_ref, send_sem, recv_sem,
):
    me = lax.axis_index("ctx")
    last = N_CTX - 1
    barrier = pltpu.get_barrier_semaphore()

    @pl.when(me > 0)
    def _():
        pl.semaphore_signal(barrier, inc=1, device_id={"ctx": me - 1}, device_id_type=MESH)

    @pl.when(me < last)
    def _():
        pl.semaphore_signal(barrier, inc=1, device_id={"ctx": me + 1}, device_id_type=MESH)

    rows = lax.broadcasted_iota(jnp.int32, (T, T), 0)
    cols = lax.broadcasted_iota(jnp.int32, (T, T), 1)
    lower = (rows >= cols).astype(F32)
    upper = (rows <= cols).astype(F32)
    eye = (rows == cols).astype(F32)
    lc_ref[...] = jnp.dot(lower, jnp.log(d_ref[...]), precision=HIGHEST, preferred_element_type=F32)
    lr_ref[...] = jnp.dot(jnp.log(dt_ref[...]), upper, precision=HIGHEST, preferred_element_type=F32)
    ones = jnp.ones((8, DK), F32)
    head_lane = lax.broadcasted_iota(jnp.int32, (T, HEADS), 1)
    in_16 = (rows // 16 == cols // 16) & (rows > cols)

    def column(array, h):
        return jnp.sum(jnp.where(head_lane == h, array, 0.0), axis=1, keepdims=True)

    def maps(step, carry):
        groups = [step * 2, step * 2 + 1]
        per_group = []
        for g in groups:
            at = pl.ds(pl.multiple_of(g * DK, DK), DK)
            kraw, qraw = k_ref[:, at], q_ref[:, at]
            kf, qf = kraw.astype(F32), qraw.astype(F32)
            ksq = kf * kf
            rk = lax.rsqrt(jnp.sum(ksq, axis=1, keepdims=True) + 1e-06)
            rk_row = lax.rsqrt(
                lax.dot_general(
                    ones, ksq, (((1,), (1,)), ((), ())), precision=HIGHEST, preferred_element_type=F32
                )[0:1] + 1e-06
            )
            rq = lax.rsqrt(jnp.sum(qf * qf, axis=1, keepdims=True) + 1e-06) * DK ** (-0.5)
            kk = mm_t(kraw, kraw) * rk * rk_row
            qk = mm_t(qraw, kraw) * rq * rk_row
            kt = kf.T * rk_row
            per_group.append((kraw, qf * rq, rk_row, kk, qk, kt))
        heads = []
        for i, g in enumerate(groups):
            for j in range(2):
                heads.append((per_group[i], g * 2 + j))
        state = []
        for (kraw, qu, rk_row, kk, qk, kt), h in heads:
            lcol = column(lc_ref[...], h)
            wcol = column(w_ref[...], h)
            lrow = lr_ref[pl.ds(h, 1), :]
            wrow = wt_ref[pl.ds(h, 1), :]
            ratio = jnp.exp(jnp.minimum(lcol - lrow, 0.0)) * lower
            a = jnp.where(rows > cols, ratio * kk, 0.0) * wcol
            remain = jnp.exp(lrow[:, T - 1 : T] - lrow)
            g2 = jnp.concatenate([qk * ratio, kt * remain], axis=0)
            state.append((a, g2, wrow, wrow * jnp.exp(lrow) * rk_row, jnp.exp(lcol)))
        n = range(len(heads))
        a = [s[0] for s in state]
        dg = [jnp.where(in_16, x, 0.0) for x in a]
        d2 = [mm(x, x) for x in dg]
        d3 = [mm(dg[i], d2[i]) for i in n]
        d4 = [mm(x, x) for x in d2]
        m1 = [eye - dg[i] + d2[i] - d3[i] for i in n]
        d8 = [mm(x, x) for x in d4]
        m2 = [m1[i] + mm(m1[i], d4[i]) for i in n]
        inv = [m2[i] + mm(m2[i], d8[i]) for i in n]
        for size in (16, 32, 64):
            band = (rows // (2 * size) == cols // (2 * size)) & (rows // size > cols // size)
            part = [jnp.where(band, x, 0.0) for x in a]
            half = [mm(part[i], inv[i]) for i in n]
            inv = [inv[i] - mm(inv[i], half[i]) for i in n]
        y = [mm(state[i][1], inv[i], 2, 2) for i in n]
        for i in n:
            (kraw, qu, rk_row, kk, qk, kt), h = heads[i]
            _, _, w1, w2, cum = state[i]
            vraw = v_ref[:, pl.ds(pl.multiple_of(h * DV, DV), DV)]
            z1 = mm(y[i] * w1, vraw, 2)
            z2 = mm(y[i] * w2, kraw, 2)
            loc_ref[h] = z1[:T]
            off_ref[h] = z1[T:]
            qeff_ref[h] = cum * qu - z2[:T]
            car_ref[h] = z2[T:]
        return carry

    lax.fori_loop(0, KH // 2, maps, 0)

    @pl.when((me > 0) & (me < last))
    def _():
        pl.semaphore_wait(barrier, 2)

    @pl.when((me == 0) | (me == last))
    def _():
        pl.semaphore_wait(barrier, 1)

    def hop(h):
        return pltpu.make_async_remote_copy(
            src_ref=sent_ref.at[h],
            dst_ref=got_ref.at[h],
            send_sem=send_sem.at[h],
            recv_sem=recv_sem.at[h],
            device_id={"ctx": jnp.minimum(me + 1, last)},
            device_id_type=MESH,
        )

    def fraction(h):
        return jnp.exp(lr_ref[pl.ds(h, 1), T - 1 : T])

    @pl.when(me == 0)
    def _():
        def start(h, carry):
            got_ref[h] = jnp.zeros((DK, DV), STATE)
            sent_ref[h] = off_ref[h].astype(STATE)
            hop(h).start()
            return carry

        lax.fori_loop(0, HEADS, start, 0)

    @pl.when((me > 0) & (me < last))
    def _():
        def relay(h, carry):
            hop(h).wait_recv()
            s = got_ref[h].astype(F32)
            sent_ref[h] = (fraction(h) * s + off_ref[h] - mm(car_ref[h], s, 2, 2)).astype(STATE)
            hop(h).start()
            return carry

        lax.fori_loop(0, HEADS, relay, 0)

    gain = gain_ref[...]

    def finish(h, carry):
        @pl.when(me == last)
        def _():
            hop(h).wait_recv()

        o = loc_ref[h] + mm(qeff_ref[h], got_ref[h].astype(F32), 2, 2)
        at = pl.ds(pl.multiple_of(h * DV, DV), DV)
        gate = gate_ref[:, at].astype(F32)
        scale = lax.rsqrt(jnp.mean(o * o, axis=1, keepdims=True) + 1e-06)
        out_ref[:, at] = (o * scale * gain * (gate / (1.0 + jnp.exp(-gate)))).astype(BF16)
        return carry

    lax.fori_loop(0, HEADS, finish, 0)

    @pl.when(me < last)
    def _():
        def drain(h, carry):
            hop(h).wait_send()
            return carry

        lax.fori_loop(0, HEADS, drain, 0)


def mixer(queries, keys, values, out_gate, write_rate, decay, head_gain):
    square = pltpu.VMEM((HEADS, DK, DV), F32)
    return pl.pallas_call(
        mixer_kernel,
        out_shape=jax.ShapeDtypeStruct((T, HEADS * DV), BF16),
        in_specs=[pl.BlockSpec(memory_space=pltpu.VMEM)] * 9,
        out_specs=pl.BlockSpec(memory_space=pltpu.VMEM),
        scratch_shapes=[
            pltpu.VMEM((T, HEADS), F32),
            pltpu.VMEM((HEADS, T), F32),
            square, square, square, square,
            pltpu.VMEM((HEADS, DK, DV), STATE),
            pltpu.VMEM((HEADS, DK, DV), STATE),
            pltpu.SemaphoreType.DMA((HEADS,)),
            pltpu.SemaphoreType.DMA((HEADS,)),
        ],
        compiler_params=pltpu.CompilerParams(
            collective_id=0, has_side_effects=True, vmem_limit_bytes=40 * 2**20
        ),
        cost_estimate=pl.CostEstimate(flops=20 * 10**9, bytes_accessed=2 * 10**6, transcendentals=0),
        name="mixer",
    )(queries, keys, values, out_gate, write_rate, write_rate.T, decay, decay.T, head_gain[None, :])


PEERS = 32
ROWS = 16
HALF = T // 2
GROUP = PEERS * ROWS
AG_CHUNKS = (
    ((1, 0), (1, 1), (2, 0), (2, 1), (3, 0), (3, 1), (4, 0)),
    ((1, 1), (1, 0), (2, 1), (2, 0), (3, 1), (3, 0), (4, 1)),
)
RS_CHUNKS = (
    ((4, 1), (3, 0), (3, 1), (2, 0), (2, 1), (1, 0), (1, 1)),
    ((4, 0), (3, 1), (3, 0), (2, 1), (2, 0), (1, 1), (1, 0)),
)
BEHIND = {1: 1, 2: 3, 3: 5, 4: 7}
AHEAD = {1: 2, 2: 4, 3: 6, 4: 7}
OFFSETS = (0, -1, 1, -2, 2, -3, 3, 4)


def moe_kernel(
    x_ref, info_ref, wg_hbm, wu_hbm, wd_hbm, out_ref,
    xg, stage, rows, outb, ret, rs_out, rs_in, y_ref, pick, high, low, wg, wu, wd,
    w_sem, ag_send, ag_recv, in_send, in_recv, back_send, back_recv, rs_send, rs_recv,
):
    ctx = lax.axis_index("ctx")
    exp = lax.axis_index("exp")
    yy, zz = exp // 8, exp % 8
    mine = ctx * 4 + yy
    barrier = pltpu.get_barrier_semaphore()

    def peer(k):
        c, y = (ctx + k // 4) % 8, (yy + k % 4) % 4
        return c * 4 + y, {"ctx": c, "exp": y * 8 + zz}

    def along(step):
        return {"ctx": ctx, "exp": yy * 8 + (zz + step + 8) % 8}

    weights = [
        pltpu.make_async_copy(s, d, w_sem.at[i])
        for i, (s, d) in enumerate(((wg_hbm, wg), (wu_hbm, wu), (wd_hbm, wd)))
    ]
    for copy in weights:
        copy.start()

    def greet(k, carry):
        pl.semaphore_signal(barrier, inc=1, device_id=peer(k)[1], device_id_type=MESH)
        return carry

    for step in (1, -1):
        pl.semaphore_signal(barrier, inc=1, device_id=along(step), device_id_type=MESH)
    lax.fori_loop(1, PEERS, greet, 0)
    xg[0] = x_ref[...]
    pl.semaphore_wait(barrier, PEERS + 1)

    def half(h):
        return pl.ds(h * HALF, HALF)

    def gather(way, i):
        d, h = AG_CHUNKS[way][i]
        slot = (BEHIND, AHEAD)[way]
        src = x_ref.at[half(h)] if d == 1 else xg.at[slot[d - 1], half(h)]
        return pltpu.make_async_remote_copy(
            src_ref=src,
            dst_ref=xg.at[slot[d], half(h)],
            send_sem=ag_send.at[way, i],
            recv_sem=ag_recv.at[way, i],
            device_id=along((1, -1)[way]),
            device_id_type=MESH,
        )

    def pass_on(first, end):
        for i in range(first, end):
            for way in (0, 1):
                gather(way, i).wait_recv()
                if i + 2 < 7:
                    gather(way, i + 2).start()

    for i in (0, 1):
        for way in (0, 1):
            gather(way, i).start()

    row = lax.broadcasted_iota(jnp.int32, (GROUP, T), 0)
    slot_of = (row % CAP).astype(F32)
    spread = (
        lax.broadcasted_iota(jnp.int32, (GROUP, PEERS), 0) // ROWS
        == lax.broadcasted_iota(jnp.int32, (GROUP, PEERS), 1)
    )
    spread_b, spread_f = spread.astype(F32).astype(BF16), spread.astype(F32)
    earlier = (
        lax.broadcasted_iota(jnp.int32, (T, T), 0) < lax.broadcasted_iota(jnp.int32, (T, T), 1)
    ).astype(F32).astype(BF16)
    named = (lax.broadcasted_iota(jnp.int32, (PEERS, T), 0) * 8 + zz).astype(F32)

    def tables(g):
        for s in range(4):
            info = info_ref[(zz + OFFSETS[g * 4 + s] + 8) % 8]
            member = jnp.zeros((PEERS, T), F32)
            weight = jnp.zeros((PEERS, T), F32)
            for j in range(TOP):
                hit = info[j : j + 1] == named
                member = member + jnp.where(hit, 1.0, 0.0)
                weight = weight + jnp.where(hit, info[TOP + j : TOP + j + 1], 0.0)
            member_b = member.astype(BF16)
            before = jnp.dot(member_b, earlier, preferred_element_type=F32)
            here = jnp.dot(spread_b, member_b, preferred_element_type=F32)
            place = jnp.dot(spread_b, before.astype(BF16), preferred_element_type=F32)
            share = jnp.dot(spread_f, weight, precision=HIGHEST, preferred_element_type=F32)
            taken = (here > 0.5) & (place == slot_of) & (row // CAP % 4 == s)
            at = pl.ds(s * T, T)
            pick[g, :, at] = jnp.where(taken, 1.0, 0.0).astype(BF16)
            scaled = jnp.where(taken, share, 0.0).T
            top = scaled.astype(BF16)
            high[g, at, :] = top
            low[g, at, :] = (scaled - top.astype(F32)).astype(BF16)

    def tiles(body):
        def run(i, carry):
            body(pl.ds(pl.multiple_of(i * 512, 512), 512))
            return carry

        lax.fori_loop(0, D // 512, run, 0)

    def own(p):
        return pl.ds(pl.multiple_of(p * ROWS, ROWS), ROWS)

    def exchange(src, dst, send, recv, g):
        def go(k, carry):
            p, device = peer(k)
            pltpu.make_async_remote_copy(
                src_ref=src.at[g, own(p)],
                dst_ref=dst.at[g, own(mine)],
                send_sem=send.at[g],
                recv_sem=recv.at[g],
                device_id=device,
                device_id_type=MESH,
            ).start()
            return carry

        lax.fori_loop(1, PEERS, go, 0)
        dst[g, own(mine)] = src[g, own(mine)]

    def all_of(ref, sem, g):
        some = ref.at[g, pl.ds(0, GROUP - ROWS)]
        return pltpu.make_async_copy(some, some, sem.at[g])

    def dispatch(g):
        def tile(at):
            x = xg[g * 4 : g * 4 + 4, :, at].reshape(GROUP, 512)
            stage[g, :, at] = jnp.dot(pick[g], x, preferred_element_type=F32).astype(BF16)

        tiles(tile)
        exchange(stage, rows, in_send, in_recv, g)

    def experts(g):
        all_of(rows, in_recv, g).wait()

        def tile(i, carry):
            at = pl.ds(pl.multiple_of(i * 256, 256), 256)
            x = rows[g, at, :]
            gate = jnp.dot(x, wg[...], preferred_element_type=F32)
            up = jnp.dot(x, wu[...], preferred_element_type=F32)
            act = (gate / (1.0 + jnp.exp(-gate)) * up).astype(BF16)
            outb[g, at, :] = jnp.dot(act, wd[...], preferred_element_type=F32).astype(BF16)
            return carry

        lax.fori_loop(0, GROUP // 256, tile, 0)
        exchange(outb, ret, back_send, back_recv, g)

    def combine(g):
        all_of(ret, back_recv, g).wait()

        def tile(at):
            r = ret[g, :, at]
            total = jnp.dot(high[g], r, preferred_element_type=F32) + jnp.dot(
                low[g], r, preferred_element_type=F32
            )
            y_ref[g * 4 : g * 4 + 4, :, at] = total.reshape(4, T, 512)

        tiles(tile)

    tables(0)
    pass_on(0, 2)
    tables(1)
    pass_on(2, 4)
    dispatch(0)
    pass_on(4, 7)
    dispatch(1)
    for copy in weights:
        copy.wait()
    experts(0)
    experts(1)
    combine(0)
    combine(1)

    def reduce(way, i):
        return pltpu.make_async_remote_copy(
            src_ref=rs_out.at[way, i],
            dst_ref=rs_in.at[way, i],
            send_sem=rs_send.at[way, i],
            recv_sem=rs_recv.at[way, i],
            device_id=along((1, -1)[way]),
            device_id_type=MESH,
        )

    for i in range(7):
        for way in (0, 1):
            d, h = RS_CHUNKS[way][i]
            part = y_ref[(AHEAD, BEHIND)[way][d], half(h)]
            if i >= 2:
                reduce(way, i - 2).wait_recv()
                part = part + rs_in[way, i - 2].astype(F32)
            rs_out[way, i] = part.astype(BF16)
            reduce(way, i).start()
    for i in (5, 6):
        for way in (0, 1):
            reduce(way, i).wait_recv()
    for h in (0, 1):
        total = y_ref[0, half(h)]
        for way in (0, 1):
            total = total + rs_in[way, RS_CHUNKS[way].index((1, h))].astype(F32)
        out_ref[half(h)] = total

    for i in range(7):
        for way in (0, 1):
            gather(way, i).wait_send()
            reduce(way, i).wait_send()
    for g in (0, 1):
        all_of(stage, in_send, g).wait()
        all_of(outb, back_send, g).wait()


def moe(x, info, w_gate, w_up, w_down):
    group = pltpu.VMEM((2, GROUP, D), BF16)
    table = pltpu.VMEM((2, GROUP, GROUP), BF16)
    ring = pltpu.VMEM((2, 7, HALF, D), BF16)
    dma = pltpu.SemaphoreType.DMA
    vmem, anywhere = pl.BlockSpec(memory_space=pltpu.VMEM), pl.BlockSpec(memory_space=pl.ANY)
    return pl.pallas_call(
        moe_kernel,
        out_shape=jax.ShapeDtypeStruct((T, D), F32),
        in_specs=[vmem, vmem, anywhere, anywhere, anywhere],
        out_specs=vmem,
        scratch_shapes=[
            pltpu.VMEM((8, T, D), BF16),
            group, group, group, group, ring, ring,
            pltpu.VMEM((8, T, D), F32),
            table, table, table,
            pltpu.VMEM((D, 512), BF16), pltpu.VMEM((D, 512), BF16), pltpu.VMEM((512, D), BF16),
            dma((3,)), dma((2, 7)), dma((2, 7)), dma((2,)), dma((2,)), dma((2,)), dma((2,)),
            dma((2, 7)), dma((2, 7)),
        ],
        compiler_params=pltpu.CompilerParams(
            collective_id=1, has_side_effects=True, vmem_limit_bytes=62 * 2**20
        ),
        cost_estimate=pl.CostEstimate(flops=12 * 10**9, bytes_accessed=10**7, transcendentals=0),
        name="moe",
    )(x, info, w_gate, w_up, w_down)


def local(
    queries, keys, values, out_gate, write_rate, decay, head_gain, residual, out_proj, ffn_gain,
    expert_ids, route_weight, w_gate, w_up, w_down, ablate_mask, direction,
):
    mixed = mixer(queries[0], keys[0], values[0], out_gate[0], write_rate[0], decay[0], head_gain)
    projected = jnp.dot(
        mixed, lax.all_gather(out_proj, "ctx", axis=0, tiled=True), preferred_element_type=F32
    )
    hidden_sum = residual[0].astype(F32) + projected
    ffn_in = (
        hidden_sum / jnp.sqrt(jnp.mean(hidden_sum * hidden_sum, -1, keepdims=True) + 1e-06) * ffn_gain
    ).astype(BF16)
    listed = jnp.concatenate([expert_ids[0].T.astype(F32), route_weight[0].T], axis=0)
    columns = [[y * 8 + z for z in range(8)] for y in range(4)]
    info = lax.all_gather(listed, "exp", axis_index_groups=columns)
    moe_sum = moe(ffn_in, info, w_gate[0], w_up[0], w_down[0])
    combined = hidden_sum + moe_sum
    unit_dir = direction / jnp.sqrt(jnp.sum(direction * direction) + 1e-06)
    along = jnp.sum(combined * unit_dir[None, :], axis=1)
    mask_f = ablate_mask[0].astype(F32)
    layer_out = combined - (mask_f * along)[:, None] * unit_dir[None, :]
    return layer_out.astype(BF16)[None]


def solution(mesh):
    tokens = P("exp", "ctx", None)
    experts = P(("ctx", "exp"), None, None)
    placed = (
        tokens, tokens, tokens, tokens, tokens, tokens, P(), tokens, P("ctx", None), P(),
        tokens, tokens, experts, experts, experts, P("exp", "ctx"), P(),
    )
    return jax.shard_map(local, mesh=mesh, in_specs=placed, out_specs=tokens, check_vma=False)
```

```python
import jax
import jax.numpy as jnp
from jax import lax
from jax.experimental import pallas as pl
from jax.experimental.pallas import tpu as pltpu
from jax.sharding import PartitionSpec as P

D = 2048
HEADS = 16
KH = 8
DK = 128
DV = 128
T = 128
TOP = 10
CAP = 4
N_CTX = 8
STATE = jnp.float32
F32 = jnp.float32
BF16 = jnp.bfloat16
HIGHEST = lax.Precision.HIGHEST
MESH = pl.DeviceIdType.MESH


def split(a, parts):
    if a.dtype == BF16:
        return [a]
    pieces = []
    for _ in range(parts):
        piece = a.astype(BF16)
        pieces.append(piece)
        a = a - piece.astype(F32)
    return pieces


def mm(a, b, na=1, nb=1):
    total = None
    for i, x in enumerate(split(a, na)):
        for j, y in enumerate(split(b, nb)):
            if i + j < max(na, nb):
                term = jnp.dot(x, y, preferred_element_type=F32)
                total = term if total is None else total + term
    return total


def mm_t(a, b):
    return lax.dot_general(a, b, (((1,), (1,)), ((), ())), preferred_element_type=F32)


def mixer_kernel(
    q_ref, k_ref, v_ref, gate_ref, w_ref, wt_ref, d_ref, dt_ref, gain_ref,
    res_ref, proj_ref, norm_ref, info_ref, hidden_ref, x_ref, infos_ref,
    lc_ref, lr_ref, loc_ref, qeff_ref, car_ref, off_ref, got_ref, sent_ref, out_ref, wo, infos,
    send_sem, recv_sem, wo_send, wo_recv, info_send, info_recv,
):
    me = lax.axis_index("ctx")
    exp = lax.axis_index("exp")
    yy, zz = exp // 8, exp % 8
    last = N_CTX - 1
    barrier = pltpu.get_barrier_semaphore()

    def column_peer(k):
        return {"ctx": me, "exp": yy * 8 + (zz + k) % 8}

    def chain_peer(step):
        return {"ctx": (me + step + 8) % 8, "exp": exp}

    @pl.when(me > 0)
    def _():
        pl.semaphore_signal(barrier, inc=1, device_id=chain_peer(-1), device_id_type=MESH)

    @pl.when(me < last)
    def _():
        pl.semaphore_signal(barrier, inc=1, device_id=chain_peer(1), device_id_type=MESH)

    for step in (2, -2):
        pl.semaphore_signal(barrier, inc=1, device_id=chain_peer(step), device_id_type=MESH)
    for k in range(1, 8):
        pl.semaphore_signal(barrier, inc=1, device_id=column_peer(k), device_id_type=MESH)

    left, right, opposite = (me + 6) % 8, (me + 2) % 8, (me + 4) % 8
    partner = {"ctx": me + 1 - 2 * (me % 2), "exp": exp}
    routes = (
        (None, me, 0, chain_peer(2)), (None, me, 1, chain_peer(2)),
        (None, me, 0, chain_peer(-2)), (None, me, 1, chain_peer(-2)),
        (None, me, 0, partner), (None, me, 1, partner),
        (left, left, 0, chain_peer(2)), (right, right, 1, chain_peer(-2)),
        (left, left, 0, partner), (left, left, 1, partner),
        (right, right, 0, partner), (right, right, 1, partner),
        (opposite, opposite, 0, partner), (opposite, opposite, 1, partner),
    )

    def shard(n):
        held, index, h, device = routes[n]
        at = pl.ds(h * 128, 128)
        return pltpu.make_async_remote_copy(
            src_ref=proj_ref.at[at] if held is None else wo.at[held, at],
            dst_ref=wo.at[index, at],
            send_sem=wo_send.at[n],
            recv_sem=wo_recv.at[n],
            device_id=device,
            device_id_type=MESH,
        )

    rows = lax.broadcasted_iota(jnp.int32, (T, T), 0)
    cols = lax.broadcasted_iota(jnp.int32, (T, T), 1)
    lower = (rows >= cols).astype(F32)
    upper = (rows <= cols).astype(F32)
    eye = (rows == cols).astype(F32)
    lc_ref[...] = jnp.dot(lower, jnp.log(d_ref[...]), precision=HIGHEST, preferred_element_type=F32)
    lr_ref[...] = jnp.dot(jnp.log(dt_ref[...]), upper, precision=HIGHEST, preferred_element_type=F32)
    ones = jnp.ones((8, DK), F32)
    head_lane = lax.broadcasted_iota(jnp.int32, (T, HEADS), 1)

    @pl.when((me > 0) & (me < last))
    def _():
        pl.semaphore_wait(barrier, 11)

    @pl.when((me == 0) | (me == last))
    def _():
        pl.semaphore_wait(barrier, 10)

    for k in range(1, 8):
        pltpu.make_async_remote_copy(
            src_ref=info_ref,
            dst_ref=infos.at[zz],
            send_sem=info_send,
            recv_sem=info_recv,
            device_id=column_peer(k),
            device_id_type=MESH,
        ).start()
    for n in (0, 3, 1, 2, 4, 5):
        shard(n).start()
    infos[zz] = info_ref[...]
    wo[me] = proj_ref[...]
    in_16 = (rows // 16 == cols // 16) & (rows > cols)

    def column(array, h):
        return jnp.sum(jnp.where(head_lane == h, array, 0.0), axis=1, keepdims=True)

    def maps(step, carry):
        groups = [step * 2, step * 2 + 1]
        per_group = []
        for g in groups:
            at = pl.ds(pl.multiple_of(g * DK, DK), DK)
            kraw, qraw = k_ref[:, at], q_ref[:, at]
            kf, qf = kraw.astype(F32), qraw.astype(F32)
            ksq = kf * kf
            rk = lax.rsqrt(jnp.sum(ksq, axis=1, keepdims=True) + 1e-06)
            rk_row = lax.rsqrt(
                lax.dot_general(
                    ones, ksq, (((1,), (1,)), ((), ())), precision=HIGHEST, preferred_element_type=F32
                )[0:1] + 1e-06
            )
            rq = lax.rsqrt(jnp.sum(qf * qf, axis=1, keepdims=True) + 1e-06) * DK ** (-0.5)
            kk = mm_t(kraw, kraw) * rk * rk_row
            qk = mm_t(qraw, kraw) * rq * rk_row
            kt = kf.T * rk_row
            per_group.append((kraw, qf * rq, rk_row, kk, qk, kt))
        heads = []
        for i, g in enumerate(groups):
            for j in range(2):
                heads.append((per_group[i], g * 2 + j))
        state = []
        for (kraw, qu, rk_row, kk, qk, kt), h in heads:
            lcol = column(lc_ref[...], h)
            wcol = column(w_ref[...], h)
            lrow = lr_ref[pl.ds(h, 1), :]
            wrow = wt_ref[pl.ds(h, 1), :]
            ratio = jnp.exp(jnp.minimum(lcol - lrow, 0.0)) * lower
            a = jnp.where(rows > cols, ratio * kk, 0.0) * wcol
            remain = jnp.exp(lrow[:, T - 1 : T] - lrow)
            g2 = jnp.concatenate([qk * ratio, kt * remain], axis=0)
            state.append((a, g2, wrow, wrow * jnp.exp(lrow) * rk_row, jnp.exp(lcol)))
        n = range(len(heads))
        a = [s[0] for s in state]
        dg = [jnp.where(in_16, x, 0.0) for x in a]
        d2 = [mm(x, x) for x in dg]
        d3 = [mm(dg[i], d2[i]) for i in n]
        d4 = [mm(x, x) for x in d2]
        m1 = [eye - dg[i] + d2[i] - d3[i] for i in n]
        d8 = [mm(x, x) for x in d4]
        m2 = [m1[i] + mm(m1[i], d4[i]) for i in n]
        inv = [m2[i] + mm(m2[i], d8[i]) for i in n]
        for size in (16, 32, 64):
            band = (rows // (2 * size) == cols // (2 * size)) & (rows // size > cols // size)
            part = [jnp.where(band, x, 0.0) for x in a]
            half = [mm(part[i], inv[i]) for i in n]
            inv = [inv[i] - mm(inv[i], half[i]) for i in n]
        y = [mm(state[i][1], inv[i], 2, 2) for i in n]
        for i in n:
            (kraw, qu, rk_row, kk, qk, kt), h = heads[i]
            _, _, w1, w2, cum = state[i]
            vraw = v_ref[:, pl.ds(pl.multiple_of(h * DV, DV), DV)]
            z1 = mm(y[i] * w1, vraw, 2)
            z2 = mm(y[i] * w2, kraw, 2)
            loc_ref[h] = z1[:T]
            off_ref[h] = z1[T:]
            qeff_ref[h] = cum * qu - z2[:T]
            car_ref[h] = z2[T:]
        return carry

    lax.fori_loop(0, KH // 2, maps, 0)

    shard(0).wait_recv()
    shard(6).start()
    shard(3).wait_recv()
    shard(7).start()

    def hop(h):
        return pltpu.make_async_remote_copy(
            src_ref=sent_ref.at[h],
            dst_ref=got_ref.at[h],
            send_sem=send_sem.at[h],
            recv_sem=recv_sem.at[h],
            device_id={"ctx": jnp.minimum(me + 1, last), "exp": exp},
            device_id_type=MESH,
        )

    def fraction(h):
        return jnp.exp(lr_ref[pl.ds(h, 1), T - 1 : T])

    @pl.when(me == 0)
    def _():
        def start(h, carry):
            got_ref[h] = jnp.zeros((DK, DV), STATE)
            sent_ref[h] = off_ref[h].astype(STATE)
            hop(h).start()
            return carry

        lax.fori_loop(0, HEADS, start, 0)

    @pl.when((me > 0) & (me < last))
    def _():
        def relay(h, carry):
            hop(h).wait_recv()
            s = got_ref[h].astype(F32)
            sent_ref[h] = (fraction(h) * s + off_ref[h] - mm(car_ref[h], s, 2, 2)).astype(STATE)
            hop(h).start()
            return carry

        lax.fori_loop(0, HEADS, relay, 0)

    shard(8).start()
    shard(11).start()
    for n in (1, 2):
        shard(n).wait_recv()
    shard(9).start()
    shard(10).start()

    gain = gain_ref[...]

    def finish(h, carry):
        @pl.when(me == last)
        def _():
            hop(h).wait_recv()

        o = loc_ref[h] + mm(qeff_ref[h], got_ref[h].astype(F32), 2, 2)
        at = pl.ds(pl.multiple_of(h * DV, DV), DV)
        gate = gate_ref[:, at].astype(F32)
        scale = lax.rsqrt(jnp.mean(o * o, axis=1, keepdims=True) + 1e-06)
        out_ref[:, at] = (o * scale * gain * (gate / (1.0 + jnp.exp(-gate)))).astype(BF16)
        return carry

    lax.fori_loop(0, HEADS, finish, 0)

    for n in (6, 7):
        shard(n).wait_recv()
        shard(n + 6).start()
    for n in (4, 5, 8, 9, 10, 11, 12, 13):
        shard(n).wait_recv()

    def project(i, total):
        at = pl.ds(pl.multiple_of(i * 512, 512), 512)
        part = res_ref[:, at].astype(F32)
        for j in range(8):
            part = part + jnp.dot(
                out_ref[:, j * 256 : j * 256 + 256], wo[j, :, at], preferred_element_type=F32
            )
        hidden_ref[:, at] = part
        return total + jnp.sum(part * part, axis=1, keepdims=True)

    total = lax.fori_loop(0, D // 512, project, jnp.zeros((T, 1), F32))
    x_ref[...] = (hidden_ref[...] * lax.rsqrt(total / D + 1e-06) * norm_ref[...]).astype(BF16)
    seven = infos.at[pl.ds(0, 7)]
    pltpu.make_async_copy(seven, seven, info_recv).wait()
    pltpu.make_async_copy(seven, seven, info_send).wait()
    infos_ref[...] = infos[...]
    for n in range(14):
        shard(n).wait_send()

    @pl.when(me < last)
    def _():
        def drain(h, carry):
            hop(h).wait_send()
            return carry

        lax.fori_loop(0, HEADS, drain, 0)


def mixer(
    queries, keys, values, out_gate, write_rate, decay, head_gain, residual, out_proj, ffn_gain, listed
):
    square = pltpu.VMEM((HEADS, DK, DV), F32)
    return pl.pallas_call(
        mixer_kernel,
        out_shape=[
            jax.ShapeDtypeStruct((T, D), F32),
            jax.ShapeDtypeStruct((T, D), BF16),
            jax.ShapeDtypeStruct((8, 24, T), F32),
        ],
        in_specs=[pl.BlockSpec(memory_space=pltpu.VMEM)] * 13,
        out_specs=[pl.BlockSpec(memory_space=pltpu.VMEM)] * 3,
        scratch_shapes=[
            pltpu.VMEM((T, HEADS), F32),
            pltpu.VMEM((HEADS, T), F32),
            square, square, square, square,
            pltpu.VMEM((HEADS, DK, DV), STATE),
            pltpu.VMEM((HEADS, DK, DV), STATE),
            pltpu.VMEM((T, HEADS * DV), BF16),
            pltpu.VMEM((N_CTX, 256, D), BF16),
            pltpu.VMEM((8, 24, T), F32),
            pltpu.SemaphoreType.DMA((HEADS,)),
            pltpu.SemaphoreType.DMA((HEADS,)),
            pltpu.SemaphoreType.DMA((14,)),
            pltpu.SemaphoreType.DMA((14,)),
            pltpu.SemaphoreType.DMA,
            pltpu.SemaphoreType.DMA,
        ],
        compiler_params=pltpu.CompilerParams(
            collective_id=0, has_side_effects=True, vmem_limit_bytes=40 * 2**20
        ),
        cost_estimate=pl.CostEstimate(flops=20 * 10**9, bytes_accessed=2 * 10**6, transcendentals=0),
        name="mixer",
    )(
        queries, keys, values, out_gate, write_rate, write_rate.T, decay, decay.T, head_gain[None, :],
        residual, out_proj, ffn_gain[None, :], listed,
    )


PEERS = 32
ROWS = 16
HALF = T // 2
GROUP = PEERS * ROWS
AG_CHUNKS = (
    ((1, 0), (1, 1), (2, 0), (2, 1), (3, 0), (3, 1), (4, 0)),
    ((1, 1), (1, 0), (2, 1), (2, 0), (3, 1), (3, 0), (4, 1)),
)
RS_CHUNKS = (
    ((4, 1), (3, 0), (3, 1), (2, 0), (2, 1), (1, 0), (1, 1)),
    ((4, 0), (3, 1), (3, 0), (2, 1), (2, 0), (1, 1), (1, 0)),
)
BEHIND = {1: 1, 2: 3, 3: 5, 4: 7}
AHEAD = {1: 2, 2: 4, 3: 6, 4: 7}
OFFSETS = (0, -1, 1, -2, 2, -3, 3, 4)


def moe_kernel(
    x_ref, info_ref, wg_hbm, wu_hbm, wd_hbm, out_ref,
    xg, stage, rows, outb, ret, rs_out, rs_in, y_ref, pick, high, low, wg, wu, wd,
    w_sem, ag_send, ag_recv, in_send, in_recv, back_send, back_recv, rs_send, rs_recv,
):
    ctx = lax.axis_index("ctx")
    exp = lax.axis_index("exp")
    yy, zz = exp // 8, exp % 8
    mine = ctx * 4 + yy
    barrier = pltpu.get_barrier_semaphore()

    def peer(k):
        c, y = (ctx + k // 4) % 8, (yy + k % 4) % 4
        return c * 4 + y, {"ctx": c, "exp": y * 8 + zz}

    def along(step):
        return {"ctx": ctx, "exp": yy * 8 + (zz + step + 8) % 8}

    weights = [
        pltpu.make_async_copy(s, d, w_sem.at[i])
        for i, (s, d) in enumerate(((wg_hbm, wg), (wu_hbm, wu), (wd_hbm, wd)))
    ]
    for copy in weights:
        copy.start()

    def greet(k, carry):
        pl.semaphore_signal(barrier, inc=1, device_id=peer(k)[1], device_id_type=MESH)
        return carry

    for step in (1, -1):
        pl.semaphore_signal(barrier, inc=1, device_id=along(step), device_id_type=MESH)
    lax.fori_loop(1, PEERS, greet, 0)
    xg[0] = x_ref[...]
    pl.semaphore_wait(barrier, PEERS + 1)

    def half(h):
        return pl.ds(h * HALF, HALF)

    def gather(way, i):
        d, h = AG_CHUNKS[way][i]
        slot = (BEHIND, AHEAD)[way]
        src = x_ref.at[half(h)] if d == 1 else xg.at[slot[d - 1], half(h)]
        return pltpu.make_async_remote_copy(
            src_ref=src,
            dst_ref=xg.at[slot[d], half(h)],
            send_sem=ag_send.at[way, i],
            recv_sem=ag_recv.at[way, i],
            device_id=along((1, -1)[way]),
            device_id_type=MESH,
        )

    def pass_on(first, end):
        for i in range(first, end):
            for way in (0, 1):
                gather(way, i).wait_recv()
                if i + 2 < 7:
                    gather(way, i + 2).start()

    for i in (0, 1):
        for way in (0, 1):
            gather(way, i).start()

    row = lax.broadcasted_iota(jnp.int32, (GROUP, T), 0)
    slot_of = (row % CAP).astype(F32)
    spread = (
        lax.broadcasted_iota(jnp.int32, (GROUP, PEERS), 0) // ROWS
        == lax.broadcasted_iota(jnp.int32, (GROUP, PEERS), 1)
    )
    spread_b, spread_f = spread.astype(F32).astype(BF16), spread.astype(F32)
    earlier = (
        lax.broadcasted_iota(jnp.int32, (T, T), 0) < lax.broadcasted_iota(jnp.int32, (T, T), 1)
    ).astype(F32).astype(BF16)
    named = (lax.broadcasted_iota(jnp.int32, (PEERS, T), 0) * 8 + zz).astype(F32)

    def tables(g):
        for s in range(4):
            info = info_ref[(zz + OFFSETS[g * 4 + s] + 8) % 8]
            member = jnp.zeros((PEERS, T), F32)
            weight = jnp.zeros((PEERS, T), F32)
            for j in range(TOP):
                hit = info[j : j + 1] == named
                member = member + jnp.where(hit, 1.0, 0.0)
                weight = weight + jnp.where(hit, info[TOP + j : TOP + j + 1], 0.0)
            member_b = member.astype(BF16)
            before = jnp.dot(member_b, earlier, preferred_element_type=F32)
            here = jnp.dot(spread_b, member_b, preferred_element_type=F32)
            place = jnp.dot(spread_b, before.astype(BF16), preferred_element_type=F32)
            share = jnp.dot(spread_f, weight, precision=HIGHEST, preferred_element_type=F32)
            taken = (here > 0.5) & (place == slot_of) & (row // CAP % 4 == s)
            at = pl.ds(s * T, T)
            pick[g, :, at] = jnp.where(taken, 1.0, 0.0).astype(BF16)
            scaled = jnp.where(taken, share, 0.0).T
            top = scaled.astype(BF16)
            high[g, at, :] = top
            low[g, at, :] = (scaled - top.astype(F32)).astype(BF16)

    def tiles(body):
        def run(i, carry):
            body(pl.ds(pl.multiple_of(i * 512, 512), 512))
            return carry

        lax.fori_loop(0, D // 512, run, 0)

    def own(p):
        return pl.ds(pl.multiple_of(p * ROWS, ROWS), ROWS)

    def exchange(src, dst, send, recv, g):
        def go(k, carry):
            p, device = peer(k)
            pltpu.make_async_remote_copy(
                src_ref=src.at[g, own(p)],
                dst_ref=dst.at[g, own(mine)],
                send_sem=send.at[g],
                recv_sem=recv.at[g],
                device_id=device,
                device_id_type=MESH,
            ).start()
            return carry

        lax.fori_loop(1, PEERS, go, 0)
        dst[g, own(mine)] = src[g, own(mine)]

    def all_of(ref, sem, g):
        some = ref.at[g, pl.ds(0, GROUP - ROWS)]
        return pltpu.make_async_copy(some, some, sem.at[g])

    def dispatch(g):
        def tile(at):
            x = xg[g * 4 : g * 4 + 4, :, at].reshape(GROUP, 512)
            stage[g, :, at] = jnp.dot(pick[g], x, preferred_element_type=F32).astype(BF16)

        tiles(tile)
        exchange(stage, rows, in_send, in_recv, g)

    def experts(g):
        all_of(rows, in_recv, g).wait()

        def tile(i, carry):
            at = pl.ds(pl.multiple_of(i * 256, 256), 256)
            x = rows[g, at, :]
            gate = jnp.dot(x, wg[...], preferred_element_type=F32)
            up = jnp.dot(x, wu[...], preferred_element_type=F32)
            act = (gate / (1.0 + jnp.exp(-gate)) * up).astype(BF16)
            outb[g, at, :] = jnp.dot(act, wd[...], preferred_element_type=F32).astype(BF16)
            return carry

        lax.fori_loop(0, GROUP // 256, tile, 0)
        exchange(outb, ret, back_send, back_recv, g)

    def combine(g):
        all_of(ret, back_recv, g).wait()

        def tile(at):
            r = ret[g, :, at]
            total = jnp.dot(high[g], r, preferred_element_type=F32) + jnp.dot(
                low[g], r, preferred_element_type=F32
            )
            y_ref[g * 4 : g * 4 + 4, :, at] = total.reshape(4, T, 512)

        tiles(tile)

    tables(0)
    pass_on(0, 2)
    tables(1)
    pass_on(2, 4)
    dispatch(0)
    pass_on(4, 7)
    dispatch(1)
    for copy in weights:
        copy.wait()
    experts(0)
    experts(1)
    combine(0)
    combine(1)

    def reduce(way, i):
        return pltpu.make_async_remote_copy(
            src_ref=rs_out.at[way, i],
            dst_ref=rs_in.at[way, i],
            send_sem=rs_send.at[way, i],
            recv_sem=rs_recv.at[way, i],
            device_id=along((1, -1)[way]),
            device_id_type=MESH,
        )

    for i in range(7):
        for way in (0, 1):
            d, h = RS_CHUNKS[way][i]
            part = y_ref[(AHEAD, BEHIND)[way][d], half(h)]
            if i >= 2:
                reduce(way, i - 2).wait_recv()
                part = part + rs_in[way, i - 2].astype(F32)
            rs_out[way, i] = part.astype(BF16)
            reduce(way, i).start()
    for i in (5, 6):
        for way in (0, 1):
            reduce(way, i).wait_recv()
    for h in (0, 1):
        total = y_ref[0, half(h)]
        for way in (0, 1):
            total = total + rs_in[way, RS_CHUNKS[way].index((1, h))].astype(F32)
        out_ref[half(h)] = total

    for i in range(7):
        for way in (0, 1):
            gather(way, i).wait_send()
            reduce(way, i).wait_send()
    for g in (0, 1):
        all_of(stage, in_send, g).wait()
        all_of(outb, back_send, g).wait()


def moe(x, info, w_gate, w_up, w_down):
    group = pltpu.VMEM((2, GROUP, D), BF16)
    table = pltpu.VMEM((2, GROUP, GROUP), BF16)
    ring = pltpu.VMEM((2, 7, HALF, D), BF16)
    dma = pltpu.SemaphoreType.DMA
    vmem, anywhere = pl.BlockSpec(memory_space=pltpu.VMEM), pl.BlockSpec(memory_space=pl.ANY)
    return pl.pallas_call(
        moe_kernel,
        out_shape=jax.ShapeDtypeStruct((T, D), F32),
        in_specs=[vmem, vmem, anywhere, anywhere, anywhere],
        out_specs=vmem,
        scratch_shapes=[
            pltpu.VMEM((8, T, D), BF16),
            group, group, group, group, ring, ring,
            pltpu.VMEM((8, T, D), F32),
            table, table, table,
            pltpu.VMEM((D, 512), BF16), pltpu.VMEM((D, 512), BF16), pltpu.VMEM((512, D), BF16),
            dma((3,)), dma((2, 7)), dma((2, 7)), dma((2,)), dma((2,)), dma((2,)), dma((2,)),
            dma((2, 7)), dma((2, 7)),
        ],
        compiler_params=pltpu.CompilerParams(
            collective_id=1, has_side_effects=True, vmem_limit_bytes=62 * 2**20
        ),
        cost_estimate=pl.CostEstimate(flops=12 * 10**9, bytes_accessed=10**7, transcendentals=0),
        name="moe",
    )(x, info, w_gate, w_up, w_down)


def local(
    queries, keys, values, out_gate, write_rate, decay, head_gain, residual, out_proj, ffn_gain,
    expert_ids, route_weight, w_gate, w_up, w_down, ablate_mask, direction,
):
    listed = jnp.concatenate(
        [expert_ids[0].T.astype(F32), route_weight[0].T, jnp.zeros((4, T), F32)], axis=0
    )
    hidden_sum, ffn_in, info = mixer(
        queries[0], keys[0], values[0], out_gate[0], write_rate[0], decay[0], head_gain, residual[0],
        out_proj, ffn_gain, listed,
    )
    moe_sum = moe(ffn_in, info, w_gate[0], w_up[0], w_down[0])
    combined = hidden_sum + moe_sum
    unit_dir = direction / jnp.sqrt(jnp.sum(direction * direction) + 1e-06)
    along = jnp.sum(combined * unit_dir[None, :], axis=1)
    mask_f = ablate_mask[0].astype(F32)
    layer_out = combined - (mask_f * along)[:, None] * unit_dir[None, :]
    return layer_out.astype(BF16)[None]


def solution(mesh):
    tokens = P("exp", "ctx", None)
    experts = P(("ctx", "exp"), None, None)
    placed = (
        tokens, tokens, tokens, tokens, tokens, tokens, P(), tokens, P("ctx", None), P(),
        tokens, tokens, experts, experts, experts, P("exp", "ctx"), P(),
    )
    return jax.shard_map(local, mesh=mesh, in_specs=placed, out_specs=tokens, check_vma=False)
```

```python
import jax
import jax.numpy as jnp
from jax import lax
from jax.experimental import pallas as pl
from jax.experimental.pallas import tpu as pltpu
from jax.sharding import PartitionSpec as P

D = 2048
HEADS = 16
KH = 8
DK = 128
DV = 128
T = 128
TOP = 10
CAP = 4
N_CTX = 8
STATE = jnp.bfloat16
F32 = jnp.float32
BF16 = jnp.bfloat16
HIGHEST = lax.Precision.HIGHEST
MESH = pl.DeviceIdType.MESH


def split(a, parts):
    if a.dtype == BF16:
        return [a]
    pieces = []
    for _ in range(parts):
        piece = a.astype(BF16)
        pieces.append(piece)
        a = a - piece.astype(F32)
    return pieces


def mm(a, b, na=1, nb=1):
    total = None
    for i, x in enumerate(split(a, na)):
        for j, y in enumerate(split(b, nb)):
            if i + j < max(na, nb):
                term = jnp.dot(x, y, preferred_element_type=F32)
                total = term if total is None else total + term
    return total


def mm_t(a, b):
    return lax.dot_general(a, b, (((1,), (1,)), ((), ())), preferred_element_type=F32)


def mixer_kernel(
    q_hbm, k_hbm, v_hbm, gate_hbm, w_ref, wt_ref, d_ref, dt_ref, gain_ref,
    res_hbm, proj_hbm, norm_ref, info_ref, hidden_ref, x_ref, infos_ref,
    q_ref, k_ref, v_ref, gate_ref, res_ref, proj_ref, load_sem,
    lc_ref, lr_ref, loc_ref, qeff_ref, car_ref, off_ref, got_ref, sent_ref, out_ref, wo, infos,
    send_sem, recv_sem, wo_send, wo_recv, info_send, info_recv,
):
    me = lax.axis_index("ctx")
    exp = lax.axis_index("exp")
    yy, zz = exp // 8, exp % 8
    last = N_CTX - 1
    barrier = pltpu.get_barrier_semaphore()
    loads = [
        pltpu.make_async_copy(source, target, load_sem.at[i])
        for i, (source, target) in enumerate((
            (q_hbm, q_ref), (k_hbm, k_ref), (v_hbm, v_ref), (gate_hbm, gate_ref),
            (res_hbm, res_ref), (proj_hbm, proj_ref),
        ))
    ]
    for i in (5, 0, 1, 2, 3, 4):
        loads[i].start()

    def column_peer(k):
        return {"ctx": me, "exp": yy * 8 + (zz + k) % 8}

    def chain_peer(step):
        return {"ctx": (me + step + 8) % 8, "exp": exp}

    @pl.when(me > 0)
    def _():
        pl.semaphore_signal(barrier, inc=1, device_id=chain_peer(-1), device_id_type=MESH)

    @pl.when(me < last)
    def _():
        pl.semaphore_signal(barrier, inc=1, device_id=chain_peer(1), device_id_type=MESH)

    for step in (2, -2):
        pl.semaphore_signal(barrier, inc=1, device_id=chain_peer(step), device_id_type=MESH)
    for k in range(1, 8):
        pl.semaphore_signal(barrier, inc=1, device_id=column_peer(k), device_id_type=MESH)

    core = me % 2
    side = 1 - 2 * core
    other = me + side
    partner = {"ctx": other, "exp": exp}
    onward = chain_peer(2 * side)
    near, near_other = (me - 2 * side + 8) % 8, (other - 2 * side + 8) % 8
    far, far_other = (me + 4) % 8, (other + 4) % 8
    routes = (
        (None, me, 0, partner), (None, me, 1, partner),
        (None, me, 0, onward), (None, me, 1, onward),
        (other, other, 0, onward), (other, other, 1, onward),
        (near, near, core, onward), (near_other, near_other, core, onward),
        (near, near, 0, partner), (near, near, 1, partner),
        (near_other, near_other, 0, partner), (near_other, near_other, 1, partner),
        (far, far, core, partner), (far_other, far_other, core, partner),
    )

    def shard(n):
        held, index, h, device = routes[n]
        at = pl.ds(pl.multiple_of(h * 128, 128), 128)
        return pltpu.make_async_remote_copy(
            src_ref=proj_ref.at[at] if held is None else wo.at[held, at],
            dst_ref=wo.at[index, at],
            send_sem=wo_send.at[n],
            recv_sem=wo_recv.at[n],
            device_id=device,
            device_id_type=MESH,
        )

    rows = lax.broadcasted_iota(jnp.int32, (T, T), 0)
    cols = lax.broadcasted_iota(jnp.int32, (T, T), 1)
    lower = (rows >= cols).astype(F32)
    upper = (rows <= cols).astype(F32)
    eye = (rows == cols).astype(F32)
    lc_ref[...] = jnp.dot(lower, jnp.log(d_ref[...]), precision=HIGHEST, preferred_element_type=F32)
    lr_ref[...] = jnp.dot(jnp.log(dt_ref[...]), upper, precision=HIGHEST, preferred_element_type=F32)
    ones = jnp.ones((8, DK), F32)
    head_lane = lax.broadcasted_iota(jnp.int32, (T, HEADS), 1)

    @pl.when((me > 0) & (me < last))
    def _():
        pl.semaphore_wait(barrier, 11)

    @pl.when((me == 0) | (me == last))
    def _():
        pl.semaphore_wait(barrier, 10)

    for k in range(1, 8):
        pltpu.make_async_remote_copy(
            src_ref=info_ref,
            dst_ref=infos.at[zz],
            send_sem=info_send,
            recv_sem=info_recv,
            device_id=column_peer(k),
            device_id_type=MESH,
        ).start()
    loads[5].wait()
    for n in (2, 3, 0, 1):
        shard(n).start()
    infos[zz] = info_ref[...]
    wo[me] = proj_ref[...]
    for i in (0, 1, 2):
        loads[i].wait()
    in_16 = (rows // 16 == cols // 16) & (rows > cols)

    def column(array, h):
        return jnp.sum(jnp.where(head_lane == h, array, 0.0), axis=1, keepdims=True)

    def maps(step, carry):
        @pl.when(step == 1)
        def _():
            for n in (0, 1):
                shard(n).wait_recv()
            for n in (4, 5):
                shard(n).start()

        groups = [step * 2, step * 2 + 1]
        per_group = []
        for g in groups:
            at = pl.ds(pl.multiple_of(g * DK, DK), DK)
            kraw, qraw = k_ref[:, at], q_ref[:, at]
            kf, qf = kraw.astype(F32), qraw.astype(F32)
            ksq = kf * kf
            rk = lax.rsqrt(jnp.sum(ksq, axis=1, keepdims=True) + 1e-06)
            rk_row = lax.rsqrt(
                lax.dot_general(
                    ones, ksq, (((1,), (1,)), ((), ())), precision=HIGHEST, preferred_element_type=F32
                )[0:1] + 1e-06
            )
            rq = lax.rsqrt(jnp.sum(qf * qf, axis=1, keepdims=True) + 1e-06) * DK ** (-0.5)
            kk = mm_t(kraw, kraw) * rk * rk_row
            qk = mm_t(qraw, kraw) * rq * rk_row
            kt = kf.T * rk_row
            per_group.append((kraw, qf * rq, rk_row, kk, qk, kt))
        heads = []
        for i, g in enumerate(groups):
            for j in range(2):
                heads.append((per_group[i], g * 2 + j))
        state = []
        for (kraw, qu, rk_row, kk, qk, kt), h in heads:
            lcol = column(lc_ref[...], h)
            wcol = column(w_ref[...], h)
            lrow = lr_ref[pl.ds(h, 1), :]
            wrow = wt_ref[pl.ds(h, 1), :]
            ratio = jnp.exp(jnp.minimum(lcol - lrow, 0.0)) * lower
            a = jnp.where(rows > cols, ratio * kk, 0.0) * wcol
            remain = jnp.exp(lrow[:, T - 1 : T] - lrow)
            g2 = jnp.concatenate([qk * ratio, kt * remain], axis=0)
            state.append((a, g2, wrow, wrow * jnp.exp(lrow) * rk_row, jnp.exp(lcol)))
        n = range(len(heads))
        a = [s[0] for s in state]
        dg = [jnp.where(in_16, x, 0.0) for x in a]
        d2 = [mm(x, x) for x in dg]
        d3 = [mm(dg[i], d2[i]) for i in n]
        d4 = [mm(x, x) for x in d2]
        m1 = [eye - dg[i] + d2[i] - d3[i] for i in n]
        d8 = [mm(x, x) for x in d4]
        m2 = [m1[i] + mm(m1[i], d4[i]) for i in n]
        inv = [m2[i] + mm(m2[i], d8[i]) for i in n]
        for size in (16, 32, 64):
            band = (rows // (2 * size) == cols // (2 * size)) & (rows // size > cols // size)
            part = [jnp.where(band, x, 0.0) for x in a]
            half = [mm(part[i], inv[i]) for i in n]
            inv = [inv[i] - mm(inv[i], half[i]) for i in n]
        y = [mm(state[i][1], inv[i], 2, 2) for i in n]
        for i in n:
            (kraw, qu, rk_row, kk, qk, kt), h = heads[i]
            _, _, w1, w2, cum = state[i]
            vraw = v_ref[:, pl.ds(pl.multiple_of(h * DV, DV), DV)]
            z1 = mm(y[i] * w1, vraw, 2)
            z2 = mm(y[i] * w2, kraw, 2)
            loc_ref[h] = z1[:T]
            off_ref[h] = z1[T:]
            qeff_ref[h] = cum * qu - z2[:T]
            car_ref[h] = z2[T:]
        return carry

    lax.fori_loop(0, KH // 2, maps, 0)

    def relieve():
        for n in (4, 5):
            shard(n).wait_recv()
        for n in (7, 10, 11):
            shard(n).start()

    for n in (2, 3):
        shard(n).wait_recv()
    for n in (6, 8, 9):
        shard(n).start()

    def hop(h):
        return pltpu.make_async_remote_copy(
            src_ref=sent_ref.at[h],
            dst_ref=got_ref.at[h],
            send_sem=send_sem.at[h],
            recv_sem=recv_sem.at[h],
            device_id={"ctx": jnp.minimum(me + 1, last), "exp": exp},
            device_id_type=MESH,
        )

    def fraction(h):
        return jnp.exp(lr_ref[pl.ds(h, 1), T - 1 : T])

    @pl.when(me == 0)
    def _():
        def start(h, carry):
            got_ref[h] = jnp.zeros((DK, DV), STATE)
            sent_ref[h] = off_ref[h].astype(STATE)
            hop(h).start()
            return carry

        lax.fori_loop(0, HEADS, start, 0)

    @pl.when((me > 0) & (me < last))
    def _():
        def relay(h, carry):
            @pl.when(h == 8)
            def _():
                relieve()

            hop(h).wait_recv()
            s = got_ref[h].astype(F32)
            sent_ref[h] = (fraction(h) * s + off_ref[h] - mm(car_ref[h], s, 2, 2)).astype(STATE)
            hop(h).start()
            return carry

        lax.fori_loop(0, HEADS, relay, 0)

    @pl.when((me == 0) | (me == last))
    def _():
        relieve()

    loads[3].wait()
    loads[4].wait()

    gain = gain_ref[...]

    def finish(h, carry):
        @pl.when(me == last)
        def _():
            hop(h).wait_recv()

        o = loc_ref[h] + mm(qeff_ref[h], got_ref[h].astype(F32), 2, 2)
        at = pl.ds(pl.multiple_of(h * DV, DV), DV)
        gate = gate_ref[:, at].astype(F32)
        scale = lax.rsqrt(jnp.mean(o * o, axis=1, keepdims=True) + 1e-06)
        out_ref[:, at] = (o * scale * gain * (gate / (1.0 + jnp.exp(-gate)))).astype(BF16)
        return carry

    lax.fori_loop(0, HEADS, finish, 0)

    for n in (6, 7):
        shard(n).wait_recv()
        shard(n + 6).start()
    for n in (8, 9, 10, 11, 12, 13):
        shard(n).wait_recv()

    def project(i, total):
        at = pl.ds(pl.multiple_of(i * 512, 512), 512)
        part = res_ref[:, at].astype(F32)
        for j in range(8):
            part = part + jnp.dot(
                out_ref[:, j * 256 : j * 256 + 256], wo[j, :, at], preferred_element_type=F32
            )
        hidden_ref[:, at] = part
        return total + jnp.sum(part * part, axis=1, keepdims=True)

    total = lax.fori_loop(0, D // 512, project, jnp.zeros((T, 1), F32))
    x_ref[...] = (hidden_ref[...] * lax.rsqrt(total / D + 1e-06) * norm_ref[...]).astype(BF16)
    seven = infos.at[pl.ds(0, 7)]
    pltpu.make_async_copy(seven, seven, info_recv).wait()
    pltpu.make_async_copy(seven, seven, info_send).wait()
    infos_ref[...] = infos[...]
    for n in range(14):
        shard(n).wait_send()

    @pl.when(me < last)
    def _():
        def drain(h, carry):
            hop(h).wait_send()
            return carry

        lax.fori_loop(0, HEADS, drain, 0)


def mixer(
    queries, keys, values, out_gate, write_rate, decay, head_gain, residual, out_proj, ffn_gain, listed
):
    square = pltpu.VMEM((HEADS, DK, DV), F32)
    return pl.pallas_call(
        mixer_kernel,
        out_shape=[
            jax.ShapeDtypeStruct((T, D), F32),
            jax.ShapeDtypeStruct((T, D), BF16),
            jax.ShapeDtypeStruct((8, 24, T), F32),
        ],
        in_specs=[
            pl.BlockSpec(memory_space=pl.ANY if i in (0, 1, 2, 3, 9, 10) else pltpu.VMEM)
            for i in range(13)
        ],
        out_specs=[pl.BlockSpec(memory_space=pltpu.VMEM)] * 3,
        scratch_shapes=[
            pltpu.VMEM((T, KH * DK), BF16),
            pltpu.VMEM((T, KH * DK), BF16),
            pltpu.VMEM((T, HEADS * DV), BF16),
            pltpu.VMEM((T, HEADS * DV), BF16),
            pltpu.VMEM((T, D), BF16),
            pltpu.VMEM((256, D), BF16),
            pltpu.SemaphoreType.DMA((6,)),
            pltpu.VMEM((T, HEADS), F32),
            pltpu.VMEM((HEADS, T), F32),
            square, square, square, square,
            pltpu.VMEM((HEADS, DK, DV), STATE),
            pltpu.VMEM((HEADS, DK, DV), STATE),
            pltpu.VMEM((T, HEADS * DV), BF16),
            pltpu.VMEM((N_CTX, 256, D), BF16),
            pltpu.VMEM((8, 24, T), F32),
            pltpu.SemaphoreType.DMA((HEADS,)),
            pltpu.SemaphoreType.DMA((HEADS,)),
            pltpu.SemaphoreType.DMA((14,)),
            pltpu.SemaphoreType.DMA((14,)),
            pltpu.SemaphoreType.DMA,
            pltpu.SemaphoreType.DMA,
        ],
        compiler_params=pltpu.CompilerParams(
            collective_id=0, has_side_effects=True, vmem_limit_bytes=62 * 2**20
        ),
        cost_estimate=pl.CostEstimate(flops=20 * 10**9, bytes_accessed=2 * 10**6, transcendentals=0),
        name="mixer",
    )(
        queries, keys, values, out_gate, write_rate, write_rate.T, decay, decay.T, head_gain[None, :],
        residual, out_proj, ffn_gain[None, :], listed,
    )


PEERS = 32
ROWS = 16
HALF = T // 2
GROUP = PEERS * ROWS
AG_CHUNKS = (
    ((1, 0), (1, 1), (2, 0), (2, 1), (3, 0), (3, 1), (4, 0)),
    ((1, 1), (1, 0), (2, 1), (2, 0), (3, 1), (3, 0), (4, 1)),
)
WIDE = D // 2
RS_CHUNKS = (
    ((4, 1), (3, 0), (3, 1), (2, 0), (2, 1), (1, 0), (1, 1)),
    ((4, 0), (3, 1), (3, 0), (2, 1), (2, 0), (1, 1), (1, 0)),
)
BEHIND = {1: 1, 2: 3, 3: 5, 4: 7}
AHEAD = {1: 2, 2: 4, 3: 6, 4: 7}
OFFSETS = (0, -1, 1, -2, 2, -3, 3, 4)


def moe_kernel(
    x_ref, info_ref, wg_hbm, wu_hbm, wd_hbm, out_ref,
    act_ref, xg, stage, rows, outb, ret, rs_out, rs_in, y_ref, pick, high, low, wg, wu, wd,
    w_sem, ag_send, ag_recv, in_send, in_recv, back_send, back_recv, rs_send, rs_recv,
):
    ctx = lax.axis_index("ctx")
    exp = lax.axis_index("exp")
    yy, zz = exp // 8, exp % 8
    mine = ctx * 4 + yy
    barrier = pltpu.get_barrier_semaphore()

    def peer(k):
        c, y = (ctx + k // 4) % 8, (yy + k % 4) % 4
        return c * 4 + y, {"ctx": c, "exp": y * 8 + zz}

    def along(step):
        return {"ctx": ctx, "exp": yy * 8 + (zz + step + 8) % 8}

    weights = [
        pltpu.make_async_copy(s, d, w_sem.at[i])
        for i, (s, d) in enumerate(((wg_hbm, wg), (wu_hbm, wu), (wd_hbm, wd)))
    ]
    for copy in weights:
        copy.start()

    def greet(k, carry):
        pl.semaphore_signal(barrier, inc=1, device_id=peer(k)[1], device_id_type=MESH)
        return carry

    for step in (1, -1):
        pl.semaphore_signal(barrier, inc=1, device_id=along(step), device_id_type=MESH)
    lax.fori_loop(1, PEERS, greet, 0)
    xg[0] = x_ref[...]
    pl.semaphore_wait(barrier, PEERS + 1)

    def half(h):
        return pl.ds(h * HALF, HALF)

    def gather(way, i):
        d, h = AG_CHUNKS[way][i]
        slot = (BEHIND, AHEAD)[way]
        src = x_ref.at[half(h)] if d == 1 else xg.at[slot[d - 1], half(h)]
        return pltpu.make_async_remote_copy(
            src_ref=src,
            dst_ref=xg.at[slot[d], half(h)],
            send_sem=ag_send.at[way, i],
            recv_sem=ag_recv.at[way, i],
            device_id=along((1, -1)[way]),
            device_id_type=MESH,
        )

    def pass_on(first, end):
        for i in range(first, end):
            for way in (0, 1):
                gather(way, i).wait_recv()
                if i + 2 < 7:
                    gather(way, i + 2).start()

    for i in (0, 1):
        for way in (0, 1):
            gather(way, i).start()

    row = lax.broadcasted_iota(jnp.int32, (GROUP, T), 0)
    slot_of = (row % CAP).astype(F32)
    spread = (
        lax.broadcasted_iota(jnp.int32, (GROUP, PEERS), 0) // ROWS
        == lax.broadcasted_iota(jnp.int32, (GROUP, PEERS), 1)
    )
    spread_b, spread_f = spread.astype(F32).astype(BF16), spread.astype(F32)
    earlier = (
        lax.broadcasted_iota(jnp.int32, (T, T), 0) < lax.broadcasted_iota(jnp.int32, (T, T), 1)
    ).astype(F32).astype(BF16)
    named = (lax.broadcasted_iota(jnp.int32, (PEERS, T), 0) * 8 + zz).astype(F32)

    def tables(g):
        for s in range(4):
            info = info_ref[(zz + OFFSETS[g * 4 + s] + 8) % 8]
            member = jnp.zeros((PEERS, T), F32)
            weight = jnp.zeros((PEERS, T), F32)
            for j in range(TOP):
                hit = info[j : j + 1] == named
                member = member + jnp.where(hit, 1.0, 0.0)
                weight = weight + jnp.where(hit, info[TOP + j : TOP + j + 1], 0.0)
            member_b = member.astype(BF16)
            before = jnp.dot(member_b, earlier, preferred_element_type=F32)
            here = jnp.dot(spread_b, member_b, preferred_element_type=F32)
            place = jnp.dot(spread_b, before.astype(BF16), preferred_element_type=F32)
            share = jnp.dot(spread_f, weight, precision=HIGHEST, preferred_element_type=F32)
            taken = (here > 0.5) & (place == slot_of) & (row // CAP % 4 == s)
            at = pl.ds(s * T, T)
            pick[g, :, at] = jnp.where(taken, 1.0, 0.0).astype(BF16)
            scaled = jnp.where(taken, share, 0.0).T
            top = scaled.astype(BF16)
            high[g, at, :] = top
            low[g, at, :] = (scaled - top.astype(F32)).astype(BF16)

    def tiles(body, first=0, end=D // 512):
        def run(i, carry):
            body(pl.ds(pl.multiple_of(i * 512, 512), 512))
            return carry

        lax.fori_loop(first, end, run, 0)

    def wide(c):
        return pl.ds(c * WIDE, WIDE)

    def own(p):
        return pl.ds(pl.multiple_of(p * ROWS, ROWS), ROWS)

    def exchange(src, dst, send, recv, g, cols):
        def go(k, carry):
            p, device = peer(k)
            pltpu.make_async_remote_copy(
                src_ref=src.at[g, own(p), cols],
                dst_ref=dst.at[g, own(mine), cols],
                send_sem=send,
                recv_sem=recv,
                device_id=device,
                device_id_type=MESH,
            ).start()
            return carry

        lax.fori_loop(1, PEERS, go, 0)
        dst[g, own(mine), cols] = src[g, own(mine), cols]

    def all_of(ref, sem, g, cols):
        some = ref.at[g, pl.ds(0, GROUP - ROWS), cols]
        return pltpu.make_async_copy(some, some, sem)

    def dispatch(g):
        def tile(at):
            x = xg[g * 4 : g * 4 + 4, :, at].reshape(GROUP, 512)
            stage[g, :, at] = jnp.dot(pick[g], x, preferred_element_type=F32).astype(BF16)

        tiles(tile)
        exchange(stage, rows, in_send.at[g], in_recv.at[g], g, pl.ds(0, D))

    def experts(g):
        all_of(rows, in_recv.at[g], g, pl.ds(0, D)).wait()

        def tile(i, carry):
            at = pl.ds(pl.multiple_of(i * 256, 256), 256)
            x = rows[g, at, :]
            gate = jnp.dot(x, wg[...], preferred_element_type=F32)
            up = jnp.dot(x, wu[...], preferred_element_type=F32)
            act_ref[at, :] = (gate / (1.0 + jnp.exp(-gate)) * up).astype(BF16)
            return carry

        lax.fori_loop(0, GROUP // 256, tile, 0)
        for c in (0, 1):
            def down(at):
                outb[g, :, at] = jnp.dot(
                    act_ref[...], wd[:, at], preferred_element_type=F32
                ).astype(BF16)

            tiles(down, 2 * c, 2 * c + 2)
            exchange(outb, ret, back_send.at[g, c], back_recv.at[g, c], g, wide(c))

    def combine(g, c):
        all_of(ret, back_recv.at[g, c], g, wide(c)).wait()

        def tile(at):
            r = ret[g, :, at]
            total = jnp.dot(high[g], r, preferred_element_type=F32) + jnp.dot(
                low[g], r, preferred_element_type=F32
            )
            y_ref[g * 4 : g * 4 + 4, :, at] = total.reshape(4, T, 512)

        tiles(tile, 2 * c, 2 * c + 2)

    tables(0)
    pass_on(0, 2)
    tables(1)
    pass_on(2, 4)
    dispatch(0)
    pass_on(4, 7)
    dispatch(1)
    for copy in weights:
        copy.wait()
    experts(0)
    experts(1)

    def reduce(c, way, i):
        return pltpu.make_async_remote_copy(
            src_ref=rs_out.at[way, i, :, wide(c)],
            dst_ref=rs_in.at[way, i, :, wide(c)],
            send_sem=rs_send.at[c, way, i],
            recv_sem=rs_recv.at[c, way, i],
            device_id=along((1, -1)[way]),
            device_id_type=MESH,
        )

    def reduce_step(c, i):
        for way in (0, 1):
            d, h = RS_CHUNKS[way][i]
            part = y_ref[(AHEAD, BEHIND)[way][d], half(h), wide(c)]
            if i >= 2:
                reduce(c, way, i - 2).wait_recv()
                part = part + rs_in[way, i - 2, :, wide(c)].astype(F32)
            rs_out[way, i, :, wide(c)] = part.astype(BF16)
            reduce(c, way, i).start()

    combine(1, 0)
    reduce_step(0, 0)
    reduce_step(0, 1)
    combine(0, 0)
    for i in range(2, 5):
        reduce_step(0, i)
    combine(1, 1)
    reduce_step(1, 0)
    reduce_step(0, 5)
    reduce_step(1, 1)
    reduce_step(0, 6)
    combine(0, 1)
    for i in range(2, 7):
        reduce_step(1, i)
    for c in (0, 1):
        for i in (5, 6):
            for way in (0, 1):
                reduce(c, way, i).wait_recv()
        for h in (0, 1):
            total = y_ref[0, half(h), wide(c)]
            for way in (0, 1):
                total = total + rs_in[way, RS_CHUNKS[way].index((1, h)), :, wide(c)].astype(F32)
            out_ref[half(h), wide(c)] = total

    for i in range(7):
        for way in (0, 1):
            gather(way, i).wait_send()
            for c in (0, 1):
                reduce(c, way, i).wait_send()
    for g in (0, 1):
        all_of(stage, in_send.at[g], g, pl.ds(0, D)).wait()
        for c in (0, 1):
            all_of(outb, back_send.at[g, c], g, wide(c)).wait()


def moe(x, info, w_gate, w_up, w_down):
    group = pltpu.VMEM((2, GROUP, D), BF16)
    table = pltpu.VMEM((2, GROUP, GROUP), BF16)
    ring = pltpu.VMEM((2, 7, HALF, D), BF16)
    dma = pltpu.SemaphoreType.DMA
    vmem, anywhere = pl.BlockSpec(memory_space=pltpu.VMEM), pl.BlockSpec(memory_space=pl.ANY)
    return pl.pallas_call(
        moe_kernel,
        out_shape=jax.ShapeDtypeStruct((T, D), F32),
        in_specs=[vmem, vmem, anywhere, anywhere, anywhere],
        out_specs=vmem,
        scratch_shapes=[
            pltpu.VMEM((GROUP, 512), BF16),
            pltpu.VMEM((8, T, D), BF16),
            group, group, group, group, ring, ring,
            pltpu.VMEM((8, T, D), F32),
            table, table, table,
            pltpu.VMEM((D, 512), BF16), pltpu.VMEM((D, 512), BF16), pltpu.VMEM((512, D), BF16),
            dma((3,)), dma((2, 7)), dma((2, 7)), dma((2,)), dma((2,)), dma((2, 2)), dma((2, 2)),
            dma((2, 2, 7)), dma((2, 2, 7)),
        ],
        compiler_params=pltpu.CompilerParams(
            collective_id=1, has_side_effects=True, vmem_limit_bytes=62 * 2**20
        ),
        cost_estimate=pl.CostEstimate(flops=12 * 10**9, bytes_accessed=10**7, transcendentals=0),
        name="moe",
    )(x, info, w_gate, w_up, w_down)


def local(
    queries, keys, values, out_gate, write_rate, decay, head_gain, residual, out_proj, ffn_gain,
    expert_ids, route_weight, w_gate, w_up, w_down, ablate_mask, direction,
):
    listed = jnp.concatenate(
        [expert_ids[0].T.astype(F32), route_weight[0].T, jnp.zeros((4, T), F32)], axis=0
    )
    hidden_sum, ffn_in, info = mixer(
        queries[0], keys[0], values[0], out_gate[0], write_rate[0], decay[0], head_gain, residual[0],
        out_proj, ffn_gain, listed,
    )
    moe_sum = moe(ffn_in, info, w_gate[0], w_up[0], w_down[0])
    combined = hidden_sum + moe_sum
    unit_dir = direction / jnp.sqrt(jnp.sum(direction * direction) + 1e-06)
    along = jnp.sum(combined * unit_dir[None, :], axis=1)
    mask_f = ablate_mask[0].astype(F32)
    layer_out = combined - (mask_f * along)[:, None] * unit_dir[None, :]
    return layer_out.astype(BF16)[None]


def solution(mesh):
    tokens = P("exp", "ctx", None)
    experts = P(("ctx", "exp"), None, None)
    placed = (
        tokens, tokens, tokens, tokens, tokens, tokens, P(), tokens, P("ctx", None), P(),
        tokens, tokens, experts, experts, experts, P("exp", "ctx"), P(),
    )
    return jax.shard_map(local, mesh=mesh, in_specs=placed, out_specs=tokens, check_vma=False)
```

```python
import jax
import jax.numpy as jnp
from jax import lax
from jax.experimental import pallas as pl
from jax.experimental.pallas import tpu as pltpu
from jax.sharding import PartitionSpec as P

D = 2048
HEADS = 16
KH = 8
DK = 128
DV = 128
T = 128
TOP = 10
CAP = 4
N_CTX = 8
STATE = jnp.bfloat16
F32 = jnp.float32
BF16 = jnp.bfloat16
HIGHEST = lax.Precision.HIGHEST
MESH = pl.DeviceIdType.MESH


def split(a, parts):
    if a.dtype == BF16:
        return [a]
    pieces = []
    for _ in range(parts):
        piece = a.astype(BF16)
        pieces.append(piece)
        a = a - piece.astype(F32)
    return pieces


def mm(a, b, na=1, nb=1):
    total = None
    for i, x in enumerate(split(a, na)):
        for j, y in enumerate(split(b, nb)):
            if i + j < max(na, nb):
                term = jnp.dot(x, y, preferred_element_type=F32)
                total = term if total is None else total + term
    return total


def mm_t(a, b):
    return lax.dot_general(a, b, (((1,), (1,)), ((), ())), preferred_element_type=F32)


def mixer_kernel(
    q_hbm, k_hbm, v_hbm, gate_hbm, wt_ref, dt_ref, gain_ref,
    res_hbm, proj_hbm, norm_ref, info_ref, hidden_ref, x_ref, infos_ref,
    q_ref, k_ref, v_ref, gate_ref, res_ref, proj_ref, load_sem,
    lc_ref, wc_ref, lr_ref, loc_ref, qeff_ref, car_ref, off_ref, got_ref, sent_ref, out_ref, wo, infos,
    send_sem, recv_sem, wo_send, wo_recv, info_send, info_recv,
):
    me = lax.axis_index("ctx")
    exp = lax.axis_index("exp")
    yy, zz = exp // 8, exp % 8
    last = N_CTX - 1
    barrier = pltpu.get_barrier_semaphore()
    loads = [
        pltpu.make_async_copy(source, target, load_sem.at[i])
        for i, (source, target) in enumerate((
            (q_hbm, q_ref), (k_hbm, k_ref), (v_hbm, v_ref), (gate_hbm, gate_ref),
            (res_hbm, res_ref), (proj_hbm, proj_ref),
        ))
    ]
    for i in (5, 0, 1, 2, 3, 4):
        loads[i].start()

    def column_peer(k):
        return {"ctx": me, "exp": yy * 8 + (zz + k) % 8}

    def chain_peer(step):
        return {"ctx": (me + step + 8) % 8, "exp": exp}

    @pl.when(me > 0)
    def _():
        pl.semaphore_signal(barrier, inc=1, device_id=chain_peer(-1), device_id_type=MESH)

    @pl.when(me < last)
    def _():
        pl.semaphore_signal(barrier, inc=1, device_id=chain_peer(1), device_id_type=MESH)

    for step in (2, -2):
        pl.semaphore_signal(barrier, inc=1, device_id=chain_peer(step), device_id_type=MESH)
    for k in range(1, 8):
        pl.semaphore_signal(barrier, inc=1, device_id=column_peer(k), device_id_type=MESH)

    core = me % 2
    side = 1 - 2 * core
    other = me + side
    partner = {"ctx": other, "exp": exp}
    onward = chain_peer(2 * side)
    near, near_other = (me - 2 * side + 8) % 8, (other - 2 * side + 8) % 8
    far, far_other = (me + 4) % 8, (other + 4) % 8
    y_mate = {"ctx": me, "exp": (yy + 1 - 2 * (yy % 2)) * 8 + zz}
    z_mate = {"ctx": me, "exp": yy * 8 + zz + 1 - 2 * (zz % 2)}
    far_mate = {
        "ctx": me,
        "exp": (yy + (1 - core) * (1 - 2 * (yy % 2))) * 8 + zz + core * (1 - 2 * (zz % 2)),
    }
    pl.semaphore_signal(barrier, inc=1, device_id=y_mate, device_id_type=MESH)
    first, second = (yy % 2) * 64, 128 + (zz % 2) * 64
    first_rest, second_rest = 64 - first, 128 + 64 - (zz % 2) * 64
    fetched = first + core * (second - first)
    rest = first_rest + core * (second_rest - first_rest)
    routes = (
        (None, me, 0, 128, partner), (None, me, 128, 128, partner),
        (None, me, first, 64, onward), (None, me, second, 64, onward),
        (other, other, first, 64, onward), (other, other, second, 64, onward),
        (near, near, fetched, 64, onward), (near_other, near_other, fetched, 64, onward),
        (near, near, first, 64, partner), (near, near, second, 64, partner),
        (near_other, near_other, first, 64, partner), (near_other, near_other, second, 64, partner),
        (far, far, fetched, 64, partner), (far_other, far_other, fetched, 64, partner),
        (near, near, first, 64, y_mate), (near, near, second, 64, z_mate),
        (near_other, near_other, first, 64, y_mate), (near_other, near_other, second, 64, z_mate),
        (far, far, fetched, 64, far_mate), (far_other, far_other, fetched, 64, far_mate),
        (near, near, first_rest, 64, partner), (near, near, second_rest, 64, partner),
        (near_other, near_other, first_rest, 64, partner),
        (near_other, near_other, second_rest, 64, partner),
        (far, far, rest, 64, partner), (far_other, far_other, rest, 64, partner),
    )

    def shard(n):
        held, index, start, size, device = routes[n]
        at = pl.ds(pl.multiple_of(start, 64), size)
        return pltpu.make_async_remote_copy(
            src_ref=proj_ref.at[at] if held is None else wo.at[held, at],
            dst_ref=wo.at[index, at],
            send_sem=wo_send.at[n],
            recv_sem=wo_recv.at[n],
            device_id=device,
            device_id_type=MESH,
        )

    def take(*numbers):
        for n in numbers:
            shard(n).wait_recv()

    def give(*numbers):
        for n in numbers:
            shard(n).start()

    rows = lax.broadcasted_iota(jnp.int32, (T, T), 0)
    cols = lax.broadcasted_iota(jnp.int32, (T, T), 1)
    lower = (rows >= cols).astype(F32)
    upper = (rows <= cols).astype(F32)
    eye = (rows == cols).astype(F32)
    by_row = (((1,), (1,)), ((), ()))
    lc_ref[...] = lax.dot_general(
        lower, jnp.log(dt_ref[...]), by_row, precision=HIGHEST, preferred_element_type=F32
    )
    wc_ref[...] = lax.dot_general(
        eye, wt_ref[...], by_row, precision=HIGHEST, preferred_element_type=F32
    )
    lr_ref[...] = jnp.dot(jnp.log(dt_ref[...]), upper, precision=HIGHEST, preferred_element_type=F32)
    ones = jnp.ones((8, DK), F32)
    head_lane = lax.broadcasted_iota(jnp.int32, (T, HEADS), 1)

    @pl.when((me > 0) & (me < last))
    def _():
        pl.semaphore_wait(barrier, 12)

    @pl.when((me == 0) | (me == last))
    def _():
        pl.semaphore_wait(barrier, 11)

    for k in range(1, 8):
        pltpu.make_async_remote_copy(
            src_ref=info_ref,
            dst_ref=infos.at[zz],
            send_sem=info_send,
            recv_sem=info_recv,
            device_id=column_peer(k),
            device_id_type=MESH,
        ).start()
    loads[5].wait()
    give(2, 3, 0, 1)
    infos[zz] = info_ref[...]
    wo[me] = proj_ref[...]
    for i in (0, 1, 2):
        loads[i].wait()
    in_16 = (rows // 16 == cols // 16) & (rows > cols)

    def column(array, h):
        return jnp.sum(jnp.where(head_lane == h, array, 0.0), axis=1, keepdims=True)

    def maps(step, carry):
        @pl.when(step == 1)
        def _():
            take(0, 1)
            give(4, 5)

        @pl.when(step == 3)
        def _():
            take(2, 3)
            give(6, 14, 15, 8, 9)

        groups = [step * 2, step * 2 + 1]
        per_group = []
        for g in groups:
            at = pl.ds(pl.multiple_of(g * DK, DK), DK)
            kraw, qraw = k_ref[:, at], q_ref[:, at]
            kf, qf = kraw.astype(F32), qraw.astype(F32)
            ksq = kf * kf
            rk = lax.rsqrt(jnp.sum(ksq, axis=1, keepdims=True) + 1e-06)
            rk_row = lax.rsqrt(
                lax.dot_general(
                    ones, ksq, (((1,), (1,)), ((), ())), precision=HIGHEST, preferred_element_type=F32
                )[0:1] + 1e-06
            )
            rq = lax.rsqrt(jnp.sum(qf * qf, axis=1, keepdims=True) + 1e-06) * DK ** (-0.5)
            kk = mm_t(kraw, kraw) * rk * rk_row
            qk = mm_t(qraw, kraw) * rq * rk_row
            kt = kf.T * rk_row
            per_group.append((kraw, qf * rq, rk_row, kk, qk, kt))
        heads = []
        for i, g in enumerate(groups):
            for j in range(2):
                heads.append((per_group[i], g * 2 + j))
        state = []
        for (kraw, qu, rk_row, kk, qk, kt), h in heads:
            lcol = column(lc_ref[...], h)
            wcol = column(wc_ref[...], h)
            lrow = lr_ref[pl.ds(h, 1), :]
            wrow = wt_ref[pl.ds(h, 1), :]
            ratio = jnp.exp(jnp.minimum(lcol - lrow, 0.0)) * lower
            a = jnp.where(rows > cols, ratio * kk, 0.0) * wcol
            remain = jnp.exp(lrow[:, T - 1 : T] - lrow)
            g2 = jnp.concatenate([qk * ratio, kt * remain], axis=0)
            state.append((a, g2, wrow, wrow * jnp.exp(lrow) * rk_row, jnp.exp(lcol)))
        n = range(len(heads))
        a = [s[0] for s in state]
        dg = [jnp.where(in_16, x, 0.0) for x in a]
        d2 = [mm(x, x) for x in dg]
        d3 = [mm(dg[i], d2[i]) for i in n]
        d4 = [mm(x, x) for x in d2]
        m1 = [eye - dg[i] + d2[i] - d3[i] for i in n]
        d8 = [mm(x, x) for x in d4]
        m2 = [m1[i] + mm(m1[i], d4[i]) for i in n]
        inv = [m2[i] + mm(m2[i], d8[i]) for i in n]
        for size in (16, 32, 64):
            band = (rows // (2 * size) == cols // (2 * size)) & (rows // size > cols // size)
            part = [jnp.where(band, x, 0.0) for x in a]
            half = [mm(part[i], inv[i]) for i in n]
            inv = [inv[i] - mm(inv[i], half[i]) for i in n]
        y = [mm(state[i][1], inv[i], 2, 2) for i in n]
        for i in n:
            (kraw, qu, rk_row, kk, qk, kt), h = heads[i]
            _, _, w1, w2, cum = state[i]
            vraw = v_ref[:, pl.ds(pl.multiple_of(h * DV, DV), DV)]
            z1 = mm(y[i] * w1, vraw, 2)
            z2 = mm(y[i] * w2, kraw, 2)
            loc_ref[h] = z1[:T]
            off_ref[h] = z1[T:]
            qeff_ref[h] = cum * qu - z2[:T]
            car_ref[h] = z2[T:]
        return carry

    lax.fori_loop(0, KH // 2, maps, 0)

    take(4, 5)
    give(7, 16, 17, 10, 11)

    def relieve():
        take(6, 7)
        give(18, 19, 12, 13)
        take(14, 15, 16, 17)
        give(20, 21, 22, 23)

    def hop(h):
        return pltpu.make_async_remote_copy(
            src_ref=sent_ref.at[h],
            dst_ref=got_ref.at[h],
            send_sem=send_sem.at[h],
            recv_sem=recv_sem.at[h],
            device_id={"ctx": jnp.minimum(me + 1, last), "exp": exp},
            device_id_type=MESH,
        )

    def fraction(h):
        return jnp.exp(lr_ref[pl.ds(h, 1), T - 1 : T])

    @pl.when(me == 0)
    def _():
        def start(h, carry):
            got_ref[h] = jnp.zeros((DK, DV), STATE)
            sent_ref[h] = off_ref[h].astype(STATE)
            hop(h).start()
            return carry

        lax.fori_loop(0, HEADS, start, 0)

    @pl.when((me > 0) & (me < last))
    def _():
        def relay(h, carry):
            @pl.when(h == 10)
            def _():
                relieve()

            hop(h).wait_recv()
            s = got_ref[h].astype(F32)
            sent_ref[h] = (fraction(h) * s + off_ref[h] - mm(car_ref[h], s, 2, 2)).astype(STATE)
            hop(h).start()
            return carry

        lax.fori_loop(0, HEADS, relay, 0)

    @pl.when((me == 0) | (me == last))
    def _():
        relieve()

    loads[3].wait()
    loads[4].wait()

    gain = gain_ref[...]

    def finish(h, carry):
        @pl.when(me == last)
        def _():
            hop(h).wait_recv()

        o = loc_ref[h] + mm(qeff_ref[h], got_ref[h].astype(F32), 2, 2)
        at = pl.ds(pl.multiple_of(h * DV, DV), DV)
        gate = gate_ref[:, at].astype(F32)
        scale = lax.rsqrt(jnp.mean(o * o, axis=1, keepdims=True) + 1e-06)
        out_ref[:, at] = (o * scale * gain * (gate / (1.0 + jnp.exp(-gate)))).astype(BF16)
        return carry

    lax.fori_loop(0, HEADS, finish, 0)

    take(18, 19)
    give(24, 25)
    take(*range(8, 14), *range(20, 26))

    def project(i, total):
        at = pl.ds(pl.multiple_of(i * 512, 512), 512)
        part = res_ref[:, at].astype(F32)
        for j in range(8):
            part = part + jnp.dot(
                out_ref[:, j * 256 : j * 256 + 256], wo[j, :, at], preferred_element_type=F32
            )
        hidden_ref[:, at] = part
        return total + jnp.sum(part * part, axis=1, keepdims=True)

    total = lax.fori_loop(0, D // 512, project, jnp.zeros((T, 1), F32))
    x_ref[...] = (hidden_ref[...] * lax.rsqrt(total / D + 1e-06) * norm_ref[...]).astype(BF16)
    seven = infos.at[pl.ds(0, 7)]
    pltpu.make_async_copy(seven, seven, info_recv).wait()
    pltpu.make_async_copy(seven, seven, info_send).wait()
    infos_ref[...] = infos[...]
    for n in range(26):
        shard(n).wait_send()

    @pl.when(me < last)
    def _():
        def drain(h, carry):
            hop(h).wait_send()
            return carry

        lax.fori_loop(0, HEADS, drain, 0)


def mixer(
    queries, keys, values, out_gate, write_rate, decay, head_gain, residual, out_proj, ffn_gain, listed
):
    square = pltpu.VMEM((HEADS, DK, DV), F32)
    return pl.pallas_call(
        mixer_kernel,
        out_shape=[
            jax.ShapeDtypeStruct((T, D), F32),
            jax.ShapeDtypeStruct((T, D), BF16),
            jax.ShapeDtypeStruct((8, 24, T), F32),
        ],
        in_specs=[
            pl.BlockSpec(memory_space=pl.ANY if i in (0, 1, 2, 3, 7, 8) else pltpu.VMEM)
            for i in range(11)
        ],
        out_specs=[pl.BlockSpec(memory_space=pltpu.VMEM)] * 3,
        scratch_shapes=[
            pltpu.VMEM((T, KH * DK), BF16),
            pltpu.VMEM((T, KH * DK), BF16),
            pltpu.VMEM((T, HEADS * DV), BF16),
            pltpu.VMEM((T, HEADS * DV), BF16),
            pltpu.VMEM((T, D), BF16),
            pltpu.VMEM((256, D), BF16),
            pltpu.SemaphoreType.DMA((6,)),
            pltpu.VMEM((T, HEADS), F32),
            pltpu.VMEM((T, HEADS), F32),
            pltpu.VMEM((HEADS, T), F32),
            square, square, square, square,
            pltpu.VMEM((HEADS, DK, DV), STATE),
            pltpu.VMEM((HEADS, DK, DV), STATE),
            pltpu.VMEM((T, HEADS * DV), BF16),
            pltpu.VMEM((N_CTX, 256, D), BF16),
            pltpu.VMEM((8, 24, T), F32),
            pltpu.SemaphoreType.DMA((HEADS,)),
            pltpu.SemaphoreType.DMA((HEADS,)),
            pltpu.SemaphoreType.DMA((26,)),
            pltpu.SemaphoreType.DMA((26,)),
            pltpu.SemaphoreType.DMA,
            pltpu.SemaphoreType.DMA,
        ],
        compiler_params=pltpu.CompilerParams(
            collective_id=0, has_side_effects=True, vmem_limit_bytes=62 * 2**20
        ),
        cost_estimate=pl.CostEstimate(flops=20 * 10**9, bytes_accessed=2 * 10**6, transcendentals=0),
        name="mixer",
    )(
        queries, keys, values, out_gate, write_rate.T, decay.T, head_gain[None, :],
        residual, out_proj, ffn_gain[None, :], listed,
    )


PEERS = 32
ROWS = 16
HALF = T // 2
GROUP = PEERS * ROWS
AG_CHUNKS = (
    ((1, 0), (1, 1), (2, 0), (2, 1), (3, 0), (3, 1), (4, 0)),
    ((1, 1), (1, 0), (2, 1), (2, 0), (3, 1), (3, 0), (4, 1)),
)
WIDE = D // 2
RS_CHUNKS = (
    ((4, 1), (3, 0), (3, 1), (2, 0), (2, 1), (1, 0), (1, 1)),
    ((4, 0), (3, 1), (3, 0), (2, 1), (2, 0), (1, 1), (1, 0)),
)
BEHIND = {1: 1, 2: 3, 3: 5, 4: 7}
AHEAD = {1: 2, 2: 4, 3: 6, 4: 7}
OFFSETS = (0, -1, 1, -2, 2, -3, 3, 4)


def moe_kernel(
    x_ref, info_ref, wg_hbm, wu_hbm, wd_hbm, out_ref,
    act_ref, xg, stage, rows, outb, ret, rs_out, rs_in, y_ref, pick, high, low, wg, wu, wd,
    w_sem, ag_send, ag_recv, in_send, in_recv, back_send, back_recv, rs_send, rs_recv,
):
    ctx = lax.axis_index("ctx")
    exp = lax.axis_index("exp")
    yy, zz = exp // 8, exp % 8
    mine = ctx * 4 + yy
    barrier = pltpu.get_barrier_semaphore()

    def peer(k):
        c, y = (ctx + k // 4) % 8, (yy + k % 4) % 4
        return c * 4 + y, {"ctx": c, "exp": y * 8 + zz}

    def along(step):
        return {"ctx": ctx, "exp": yy * 8 + (zz + step + 8) % 8}

    weights = [
        pltpu.make_async_copy(s, d, w_sem.at[i])
        for i, (s, d) in enumerate(((wg_hbm, wg), (wu_hbm, wu), (wd_hbm, wd)))
    ]
    for copy in weights:
        copy.start()

    def greet(k, carry):
        pl.semaphore_signal(barrier, inc=1, device_id=peer(k)[1], device_id_type=MESH)
        return carry

    for step in (1, -1):
        pl.semaphore_signal(barrier, inc=1, device_id=along(step), device_id_type=MESH)
    lax.fori_loop(1, PEERS, greet, 0)
    xg[0] = x_ref[...]
    pl.semaphore_wait(barrier, PEERS + 1)

    def half(h):
        return pl.ds(h * HALF, HALF)

    def gather(way, i):
        d, h = AG_CHUNKS[way][i]
        slot = (BEHIND, AHEAD)[way]
        src = x_ref.at[half(h)] if d == 1 else xg.at[slot[d - 1], half(h)]
        return pltpu.make_async_remote_copy(
            src_ref=src,
            dst_ref=xg.at[slot[d], half(h)],
            send_sem=ag_send.at[way, i],
            recv_sem=ag_recv.at[way, i],
            device_id=along((1, -1)[way]),
            device_id_type=MESH,
        )

    def pass_on(first, end):
        for i in range(first, end):
            for way in (0, 1):
                gather(way, i).wait_recv()
                if i + 2 < 7:
                    gather(way, i + 2).start()

    for i in (0, 1):
        for way in (0, 1):
            gather(way, i).start()

    row = lax.broadcasted_iota(jnp.int32, (GROUP, T), 0)
    slot_of = (row % CAP).astype(F32)
    spread = (
        lax.broadcasted_iota(jnp.int32, (GROUP, PEERS), 0) // ROWS
        == lax.broadcasted_iota(jnp.int32, (GROUP, PEERS), 1)
    )
    spread_b, spread_f = spread.astype(F32).astype(BF16), spread.astype(F32)
    earlier = (
        lax.broadcasted_iota(jnp.int32, (T, T), 0) < lax.broadcasted_iota(jnp.int32, (T, T), 1)
    ).astype(F32).astype(BF16)
    named = (lax.broadcasted_iota(jnp.int32, (PEERS, T), 0) * 8 + zz).astype(F32)

    def tables(g):
        for s in range(4):
            info = info_ref[(zz + OFFSETS[g * 4 + s] + 8) % 8]
            member = jnp.zeros((PEERS, T), F32)
            weight = jnp.zeros((PEERS, T), F32)
            for j in range(TOP):
                hit = info[j : j + 1] == named
                member = member + jnp.where(hit, 1.0, 0.0)
                weight = weight + jnp.where(hit, info[TOP + j : TOP + j + 1], 0.0)
            member_b = member.astype(BF16)
            before = jnp.dot(member_b, earlier, preferred_element_type=F32)
            here = jnp.dot(spread_b, member_b, preferred_element_type=F32)
            place = jnp.dot(spread_b, before.astype(BF16), preferred_element_type=F32)
            share = jnp.dot(spread_f, weight, precision=HIGHEST, preferred_element_type=F32)
            taken = (here > 0.5) & (place == slot_of) & (row // CAP % 4 == s)
            at = pl.ds(s * T, T)
            pick[g, :, at] = jnp.where(taken, 1.0, 0.0).astype(BF16)
            scaled = jnp.where(taken, share, 0.0).T
            top = scaled.astype(BF16)
            high[g, at, :] = top
            low[g, at, :] = (scaled - top.astype(F32)).astype(BF16)

    def tiles(body, first=0, end=D // 512):
        def run(i, carry):
            body(pl.ds(pl.multiple_of(i * 512, 512), 512))
            return carry

        lax.fori_loop(first, end, run, 0)

    def wide(c):
        return pl.ds(c * WIDE, WIDE)

    def own(p):
        return pl.ds(pl.multiple_of(p * ROWS, ROWS), ROWS)

    def exchange(src, dst, send, recv, g, cols):
        def go(k, carry):
            p, device = peer(k)
            pltpu.make_async_remote_copy(
                src_ref=src.at[g, own(p), cols],
                dst_ref=dst.at[g, own(mine), cols],
                send_sem=send,
                recv_sem=recv,
                device_id=device,
                device_id_type=MESH,
            ).start()
            return carry

        lax.fori_loop(1, PEERS, go, 0)
        dst[g, own(mine), cols] = src[g, own(mine), cols]

    def all_of(ref, sem, g, cols):
        some = ref.at[g, pl.ds(0, GROUP - ROWS), cols]
        return pltpu.make_async_copy(some, some, sem)

    def dispatch(g):
        def tile(at):
            x = xg[g * 4 : g * 4 + 4, :, at].reshape(GROUP, 512)
            stage[g, :, at] = jnp.dot(pick[g], x, preferred_element_type=F32).astype(BF16)

        tiles(tile)
        exchange(stage, rows, in_send.at[g], in_recv.at[g], g, pl.ds(0, D))

    def experts(g):
        all_of(rows, in_recv.at[g], g, pl.ds(0, D)).wait()

        def tile(i, carry):
            at = pl.ds(pl.multiple_of(i * 256, 256), 256)
            x = rows[g, at, :]
            gate = jnp.dot(x, wg[...], preferred_element_type=F32)
            up = jnp.dot(x, wu[...], preferred_element_type=F32)
            act_ref[at, :] = (gate / (1.0 + jnp.exp(-gate)) * up).astype(BF16)
            return carry

        lax.fori_loop(0, GROUP // 256, tile, 0)
        for c in (0, 1):
            def down(at):
                outb[g, :, at] = jnp.dot(
                    act_ref[...], wd[:, at], preferred_element_type=F32
                ).astype(BF16)

            tiles(down, 2 * c, 2 * c + 2)
            exchange(outb, ret, back_send.at[g, c], back_recv.at[g, c], g, wide(c))

    def combine(g, c):
        all_of(ret, back_recv.at[g, c], g, wide(c)).wait()

        def tile(at):
            r = ret[g, :, at]
            total = jnp.dot(high[g], r, preferred_element_type=F32) + jnp.dot(
                low[g], r, preferred_element_type=F32
            )
            y_ref[g * 4 : g * 4 + 4, :, at] = total.reshape(4, T, 512)

        tiles(tile, 2 * c, 2 * c + 2)

    tables(0)
    pass_on(0, 2)
    tables(1)
    pass_on(2, 4)
    dispatch(0)
    pass_on(4, 7)
    dispatch(1)
    for copy in weights:
        copy.wait()
    experts(0)
    experts(1)

    def reduce(c, way, i):
        return pltpu.make_async_remote_copy(
            src_ref=rs_out.at[way, i, :, wide(c)],
            dst_ref=rs_in.at[way, i, :, wide(c)],
            send_sem=rs_send.at[c, way, i],
            recv_sem=rs_recv.at[c, way, i],
            device_id=along((1, -1)[way]),
            device_id_type=MESH,
        )

    def reduce_step(c, i):
        for way in (0, 1):
            d, h = RS_CHUNKS[way][i]
            part = y_ref[(AHEAD, BEHIND)[way][d], half(h), wide(c)]
            if i >= 2:
                reduce(c, way, i - 2).wait_recv()
                part = part + rs_in[way, i - 2, :, wide(c)].astype(F32)
            rs_out[way, i, :, wide(c)] = part.astype(BF16)
            reduce(c, way, i).start()

    combine(1, 0)
    reduce_step(0, 0)
    reduce_step(0, 1)
    combine(0, 0)
    for i in range(2, 5):
        reduce_step(0, i)
    combine(1, 1)
    reduce_step(1, 0)
    reduce_step(0, 5)
    reduce_step(1, 1)
    reduce_step(0, 6)
    combine(0, 1)
    for i in range(2, 7):
        reduce_step(1, i)
    for c in (0, 1):
        for i in (5, 6):
            for way in (0, 1):
                reduce(c, way, i).wait_recv()
        for h in (0, 1):
            total = y_ref[0, half(h), wide(c)]
            for way in (0, 1):
                total = total + rs_in[way, RS_CHUNKS[way].index((1, h)), :, wide(c)].astype(F32)
            out_ref[half(h), wide(c)] = total

    for i in range(7):
        for way in (0, 1):
            gather(way, i).wait_send()
            for c in (0, 1):
                reduce(c, way, i).wait_send()
    for g in (0, 1):
        all_of(stage, in_send.at[g], g, pl.ds(0, D)).wait()
        for c in (0, 1):
            all_of(outb, back_send.at[g, c], g, wide(c)).wait()


def moe(x, info, w_gate, w_up, w_down):
    group = pltpu.VMEM((2, GROUP, D), BF16)
    table = pltpu.VMEM((2, GROUP, GROUP), BF16)
    ring = pltpu.VMEM((2, 7, HALF, D), BF16)
    dma = pltpu.SemaphoreType.DMA
    vmem, anywhere = pl.BlockSpec(memory_space=pltpu.VMEM), pl.BlockSpec(memory_space=pl.ANY)
    return pl.pallas_call(
        moe_kernel,
        out_shape=jax.ShapeDtypeStruct((T, D), F32),
        in_specs=[vmem, vmem, anywhere, anywhere, anywhere],
        out_specs=vmem,
        scratch_shapes=[
            pltpu.VMEM((GROUP, 512), BF16),
            pltpu.VMEM((8, T, D), BF16),
            group, group, group, group, ring, ring,
            pltpu.VMEM((8, T, D), F32),
            table, table, table,
            pltpu.VMEM((D, 512), BF16), pltpu.VMEM((D, 512), BF16), pltpu.VMEM((512, D), BF16),
            dma((3,)), dma((2, 7)), dma((2, 7)), dma((2,)), dma((2,)), dma((2, 2)), dma((2, 2)),
            dma((2, 2, 7)), dma((2, 2, 7)),
        ],
        compiler_params=pltpu.CompilerParams(
            collective_id=1, has_side_effects=True, vmem_limit_bytes=62 * 2**20
        ),
        cost_estimate=pl.CostEstimate(flops=12 * 10**9, bytes_accessed=10**7, transcendentals=0),
        name="moe",
    )(x, info, w_gate, w_up, w_down)


def local(
    queries, keys, values, out_gate, write_rate, decay, head_gain, residual, out_proj, ffn_gain,
    expert_ids, route_weight, w_gate, w_up, w_down, ablate_mask, direction,
):
    listed = jnp.concatenate(
        [expert_ids[0].T.astype(F32), route_weight[0].T, jnp.zeros((4, T), F32)], axis=0
    )
    hidden_sum, ffn_in, info = mixer(
        queries[0], keys[0], values[0], out_gate[0], write_rate[0], decay[0], head_gain, residual[0],
        out_proj, ffn_gain, listed,
    )
    moe_sum = moe(ffn_in, info, w_gate[0], w_up[0], w_down[0])
    combined = hidden_sum + moe_sum
    unit_dir = direction / jnp.sqrt(jnp.sum(direction * direction) + 1e-06)
    along = jnp.sum(combined * unit_dir[None, :], axis=1)
    mask_f = ablate_mask[0].astype(F32)
    layer_out = combined - (mask_f * along)[:, None] * unit_dir[None, :]
    return layer_out.astype(BF16)[None]


def solution(mesh):
    tokens = P("exp", "ctx", None)
    experts = P(("ctx", "exp"), None, None)
    placed = (
        tokens, tokens, tokens, tokens, tokens, tokens, P(), tokens, P("ctx", None), P(),
        tokens, tokens, experts, experts, experts, P("exp", "ctx"), P(),
    )
    return jax.shard_map(local, mesh=mesh, in_specs=placed, out_specs=tokens, check_vma=False)
```

```python
import jax
import jax.numpy as jnp
from jax import lax
from jax.experimental import pallas as pl
from jax.experimental.pallas import tpu as pltpu
from jax.sharding import PartitionSpec as P

D = 2048
HEADS = 16
KH = 8
DK = 128
DV = 128
T = 128
TOP = 10
CAP = 4
N_CTX = 8
STATE = jnp.bfloat16
F32 = jnp.float32
BF16 = jnp.bfloat16
HIGHEST = lax.Precision.HIGHEST
MESH = pl.DeviceIdType.MESH


def split(a, parts):
    if a.dtype == BF16:
        return [a]
    pieces = []
    for _ in range(parts):
        piece = a.astype(BF16)
        pieces.append(piece)
        a = a - piece.astype(F32)
    return pieces


def mm(a, b, na=1, nb=1):
    total = None
    for i, x in enumerate(split(a, na)):
        for j, y in enumerate(split(b, nb)):
            if i + j < max(na, nb):
                term = jnp.dot(x, y, preferred_element_type=F32)
                total = term if total is None else total + term
    return total


def mm_t(a, b):
    return lax.dot_general(a, b, (((1,), (1,)), ((), ())), preferred_element_type=F32)


def mixer_kernel(
    q_hbm, k_hbm, v_hbm, gate_hbm, wt_ref, dt_ref, gain_ref,
    res_hbm, proj_hbm, norm_ref, info_ref, hidden_ref, x_ref, infos_ref,
    q_ref, k_ref, v_ref, gate_ref, res_ref, proj_ref, load_sem,
    lc_ref, wc_ref, lr_ref, loc_ref, qeff_ref, car_ref, off_ref, got_ref, sent_ref, out_ref, wo, infos,
    send_sem, recv_sem, wo_send, wo_recv, info_send, info_recv,
):
    me = lax.axis_index("ctx")
    exp = lax.axis_index("exp")
    yy, zz = exp // 8, exp % 8
    last = N_CTX - 1
    barrier = pltpu.get_barrier_semaphore()
    loads = [
        pltpu.make_async_copy(source, target, load_sem.at[i])
        for i, (source, target) in enumerate((
            (q_hbm, q_ref), (k_hbm, k_ref), (v_hbm, v_ref), (gate_hbm, gate_ref),
            (res_hbm, res_ref), (proj_hbm, proj_ref),
        ))
    ]
    for i in (5, 0, 1, 2, 3, 4):
        loads[i].start()

    def column_peer(k):
        return {"ctx": me, "exp": yy * 8 + (zz + k) % 8}

    def chain_peer(step):
        return {"ctx": (me + step + 8) % 8, "exp": exp}

    @pl.when(me > 0)
    def _():
        pl.semaphore_signal(barrier, inc=1, device_id=chain_peer(-1), device_id_type=MESH)

    @pl.when(me < last)
    def _():
        pl.semaphore_signal(barrier, inc=1, device_id=chain_peer(1), device_id_type=MESH)

    for step in (2, -2):
        pl.semaphore_signal(barrier, inc=1, device_id=chain_peer(step), device_id_type=MESH)
    for k in range(1, 8):
        pl.semaphore_signal(barrier, inc=1, device_id=column_peer(k), device_id_type=MESH)

    core = me % 2
    side = 1 - 2 * core
    other = me + side
    partner = {"ctx": other, "exp": exp}
    onward = chain_peer(2 * side)
    near, near_other = (me - 2 * side + 8) % 8, (other - 2 * side + 8) % 8
    far, far_other = (me + 4) % 8, (other + 4) % 8
    y_mate = {"ctx": me, "exp": (yy + 1 - 2 * (yy % 2)) * 8 + zz}
    z_mate = {"ctx": me, "exp": yy * 8 + zz + 1 - 2 * (zz % 2)}
    far_mate = {
        "ctx": me,
        "exp": (yy + (1 - core) * (1 - 2 * (yy % 2))) * 8 + zz + core * (1 - 2 * (zz % 2)),
    }
    pl.semaphore_signal(barrier, inc=1, device_id=y_mate, device_id_type=MESH)
    first, second = (yy % 2) * 64, 128 + (zz % 2) * 64
    first_rest, second_rest = 64 - first, 128 + 64 - (zz % 2) * 64
    fetched = first + core * (second - first)
    rest = first_rest + core * (second_rest - first_rest)
    routes = (
        (None, me, 0, 128, partner), (None, me, 128, 128, partner),
        (None, me, first, 64, onward), (None, me, second, 64, onward),
        (other, other, first, 64, onward), (other, other, second, 64, onward),
        (near, near, fetched, 64, onward), (near_other, near_other, fetched, 64, onward),
        (near, near, first, 64, partner), (near, near, second, 64, partner),
        (near_other, near_other, first, 64, partner), (near_other, near_other, second, 64, partner),
        (far, far, fetched, 64, partner), (far_other, far_other, fetched, 64, partner),
        (near, near, first, 64, y_mate), (near, near, second, 64, z_mate),
        (near_other, near_other, first, 64, y_mate), (near_other, near_other, second, 64, z_mate),
        (far, far, fetched, 64, far_mate), (far_other, far_other, fetched, 64, far_mate),
        (near, near, first_rest, 64, partner), (near, near, second_rest, 64, partner),
        (near_other, near_other, first_rest, 64, partner),
        (near_other, near_other, second_rest, 64, partner),
        (far, far, rest, 64, partner), (far_other, far_other, rest, 64, partner),
    )

    def shard(n):
        held, index, start, size, device = routes[n]
        at = pl.ds(pl.multiple_of(start, 64), size)
        return pltpu.make_async_remote_copy(
            src_ref=proj_ref.at[at] if held is None else wo.at[held, at],
            dst_ref=wo.at[index, at],
            send_sem=wo_send.at[n],
            recv_sem=wo_recv.at[n],
            device_id=device,
            device_id_type=MESH,
        )

    def take(*numbers):
        for n in numbers:
            shard(n).wait_recv()

    def give(*numbers):
        for n in numbers:
            shard(n).start()

    rows = lax.broadcasted_iota(jnp.int32, (T, T), 0)
    cols = lax.broadcasted_iota(jnp.int32, (T, T), 1)
    lower = (rows >= cols).astype(F32)
    upper = (rows <= cols).astype(F32)
    eye = (rows == cols).astype(F32)
    by_row = (((1,), (1,)), ((), ()))
    lc_ref[...] = lax.dot_general(
        lower, jnp.log(dt_ref[...]), by_row, precision=HIGHEST, preferred_element_type=F32
    )
    wc_ref[...] = lax.dot_general(
        eye, wt_ref[...], by_row, precision=HIGHEST, preferred_element_type=F32
    )
    lr_ref[...] = jnp.dot(jnp.log(dt_ref[...]), upper, precision=HIGHEST, preferred_element_type=F32)
    ones = jnp.ones((8, DK), F32)
    head_lane = lax.broadcasted_iota(jnp.int32, (T, HEADS), 1)

    @pl.when((me > 0) & (me < last))
    def _():
        pl.semaphore_wait(barrier, 12)

    @pl.when((me == 0) | (me == last))
    def _():
        pl.semaphore_wait(barrier, 11)

    for k in range(1, 8):
        pltpu.make_async_remote_copy(
            src_ref=info_ref,
            dst_ref=infos.at[zz],
            send_sem=info_send,
            recv_sem=info_recv,
            device_id=column_peer(k),
            device_id_type=MESH,
        ).start()
    loads[5].wait()
    give(2, 3, 0, 1)
    infos[zz] = info_ref[...]
    wo[me] = proj_ref[...]
    for i in (0, 1, 2):
        loads[i].wait()
    in_16 = (rows // 16 == cols // 16) & (rows > cols)

    def column(array, h):
        return jnp.sum(jnp.where(head_lane == h, array, 0.0), axis=1, keepdims=True)

    def maps(step, carry):
        @pl.when(step == 1)
        def _():
            take(0, 1)
            give(4, 5)

        @pl.when(step == 3)
        def _():
            take(2, 3)
            give(6, 14, 15, 8, 9)

        groups = [step * 2, step * 2 + 1]
        per_group = []
        for g in groups:
            at = pl.ds(pl.multiple_of(g * DK, DK), DK)
            kraw, qraw = k_ref[:, at], q_ref[:, at]
            kf, qf = kraw.astype(F32), qraw.astype(F32)
            ksq = kf * kf
            rk = lax.rsqrt(jnp.sum(ksq, axis=1, keepdims=True) + 1e-06)
            rk_row = lax.rsqrt(
                lax.dot_general(
                    ones, ksq, (((1,), (1,)), ((), ())), precision=HIGHEST, preferred_element_type=F32
                )[0:1] + 1e-06
            )
            rq = lax.rsqrt(jnp.sum(qf * qf, axis=1, keepdims=True) + 1e-06) * DK ** (-0.5)
            kk = mm_t(kraw, kraw) * rk * rk_row
            qk = mm_t(qraw, kraw) * rq * rk_row
            kt = kf.T * rk_row
            per_group.append((kraw, qf * rq, rk_row, kk, qk, kt))
        heads = []
        for i, g in enumerate(groups):
            for j in range(2):
                heads.append((per_group[i], g * 2 + j))
        state = []
        for (kraw, qu, rk_row, kk, qk, kt), h in heads:
            lcol = column(lc_ref[...], h)
            wcol = column(wc_ref[...], h)
            lrow = lr_ref[pl.ds(h, 1), :]
            wrow = wt_ref[pl.ds(h, 1), :]
            ratio = jnp.exp(jnp.minimum(lcol - lrow, 0.0)) * lower
            a = jnp.where(rows > cols, ratio * kk, 0.0) * wcol
            remain = jnp.exp(lrow[:, T - 1 : T] - lrow)
            g2 = jnp.concatenate([qk * ratio, kt * remain], axis=0)
            state.append((a, g2, wrow, wrow * jnp.exp(lrow) * rk_row, jnp.exp(lcol)))
        n = range(len(heads))
        a = [s[0] for s in state]
        dg = [jnp.where(in_16, x, 0.0) for x in a]
        d2 = [mm(x, x) for x in dg]
        d3 = [mm(dg[i], d2[i]) for i in n]
        d4 = [mm(x, x) for x in d2]
        m1 = [eye - dg[i] + d2[i] - d3[i] for i in n]
        d8 = [mm(x, x) for x in d4]
        m2 = [m1[i] + mm(m1[i], d4[i]) for i in n]
        inv = [m2[i] + mm(m2[i], d8[i]) for i in n]
        for size in (16, 32, 64):
            band = (rows // (2 * size) == cols // (2 * size)) & (rows // size > cols // size)
            part = [jnp.where(band, x, 0.0) for x in a]
            half = [mm(part[i], inv[i]) for i in n]
            inv = [inv[i] - mm(inv[i], half[i]) for i in n]
        y = [mm(state[i][1], inv[i], 2, 2) for i in n]
        for i in n:
            (kraw, qu, rk_row, kk, qk, kt), h = heads[i]
            _, _, w1, w2, cum = state[i]
            vraw = v_ref[:, pl.ds(pl.multiple_of(h * DV, DV), DV)]
            z1 = mm(y[i] * w1, vraw, 2)
            z2 = mm(y[i] * w2, kraw, 2)
            loc_ref[h] = z1[:T]
            off_ref[h] = z1[T:]
            qeff_ref[h] = cum * qu - z2[:T]
            car_ref[h] = z2[T:]
        return carry

    lax.fori_loop(0, KH // 2, maps, 0)

    take(4, 5)
    give(7, 16, 17, 10, 11)

    def relieve():
        take(6, 7)
        give(18, 19, 12, 13)
        take(14, 15, 16, 17)
        give(20, 21, 22, 23)

    def hop(h):
        return pltpu.make_async_remote_copy(
            src_ref=sent_ref.at[h],
            dst_ref=got_ref.at[h],
            send_sem=send_sem.at[h],
            recv_sem=recv_sem.at[h],
            device_id={"ctx": jnp.minimum(me + 1, last), "exp": exp},
            device_id_type=MESH,
        )

    def fraction(h):
        return jnp.exp(lr_ref[pl.ds(h, 1), T - 1 : T])

    @pl.when(me == 0)
    def _():
        def start(h, carry):
            got_ref[h] = jnp.zeros((DK, DV), STATE)
            sent_ref[h] = off_ref[h].astype(STATE)
            hop(h).start()
            return carry

        lax.fori_loop(0, HEADS, start, 0)

    @pl.when((me > 0) & (me < last))
    def _():
        def relay(h, carry):
            @pl.when(h == 10)
            def _():
                relieve()

            hop(h).wait_recv()
            s = got_ref[h].astype(F32)
            sent_ref[h] = (fraction(h) * s + off_ref[h] - mm(car_ref[h], s, 2, 2)).astype(STATE)
            hop(h).start()
            return carry

        lax.fori_loop(0, HEADS, relay, 0)

    @pl.when((me == 0) | (me == last))
    def _():
        relieve()

    loads[3].wait()
    loads[4].wait()

    gain = gain_ref[...]

    def finish(h, carry):
        @pl.when(me == last)
        def _():
            hop(h).wait_recv()

        o = loc_ref[h] + mm(qeff_ref[h], got_ref[h].astype(F32), 2, 2)
        at = pl.ds(pl.multiple_of(h * DV, DV), DV)
        gate = gate_ref[:, at].astype(F32)
        scale = lax.rsqrt(jnp.mean(o * o, axis=1, keepdims=True) + 1e-06)
        out_ref[:, at] = (o * scale * gain * (gate / (1.0 + jnp.exp(-gate)))).astype(BF16)
        return carry

    lax.fori_loop(0, HEADS, finish, 0)

    take(18, 19)
    give(24, 25)
    take(*range(8, 14), *range(20, 26))

    def project(i, total):
        at = pl.ds(pl.multiple_of(i * 512, 512), 512)
        part = res_ref[:, at].astype(F32)
        for j in range(8):
            part = part + jnp.dot(
                out_ref[:, j * 256 : j * 256 + 256], wo[j, :, at], preferred_element_type=F32
            )
        hidden_ref[:, at] = part
        return total + jnp.sum(part * part, axis=1, keepdims=True)

    total = lax.fori_loop(0, D // 512, project, jnp.zeros((T, 1), F32))
    x_ref[...] = (hidden_ref[...] * lax.rsqrt(total / D + 1e-06) * norm_ref[...]).astype(BF16)
    seven = infos.at[pl.ds(0, 7)]
    pltpu.make_async_copy(seven, seven, info_recv).wait()
    pltpu.make_async_copy(seven, seven, info_send).wait()
    infos_ref[...] = infos[...]
    for n in range(26):
        shard(n).wait_send()

    @pl.when(me < last)
    def _():
        def drain(h, carry):
            hop(h).wait_send()
            return carry

        lax.fori_loop(0, HEADS, drain, 0)


def mixer(
    queries, keys, values, out_gate, write_rate, decay, head_gain, residual, out_proj, ffn_gain, listed
):
    square = pltpu.VMEM((HEADS, DK, DV), F32)
    return pl.pallas_call(
        mixer_kernel,
        out_shape=[
            jax.ShapeDtypeStruct((T, D), F32),
            jax.ShapeDtypeStruct((T, D), BF16),
            jax.ShapeDtypeStruct((8, 24, T), F32),
        ],
        in_specs=[
            pl.BlockSpec(memory_space=pl.ANY if i in (0, 1, 2, 3, 7, 8) else pltpu.VMEM)
            for i in range(11)
        ],
        out_specs=[pl.BlockSpec(memory_space=pltpu.VMEM)] * 3,
        scratch_shapes=[
            pltpu.VMEM((T, KH * DK), BF16),
            pltpu.VMEM((T, KH * DK), BF16),
            pltpu.VMEM((T, HEADS * DV), BF16),
            pltpu.VMEM((T, HEADS * DV), BF16),
            pltpu.VMEM((T, D), BF16),
            pltpu.VMEM((256, D), BF16),
            pltpu.SemaphoreType.DMA((6,)),
            pltpu.VMEM((T, HEADS), F32),
            pltpu.VMEM((T, HEADS), F32),
            pltpu.VMEM((HEADS, T), F32),
            square, square, square, square,
            pltpu.VMEM((HEADS, DK, DV), STATE),
            pltpu.VMEM((HEADS, DK, DV), STATE),
            pltpu.VMEM((T, HEADS * DV), BF16),
            pltpu.VMEM((N_CTX, 256, D), BF16),
            pltpu.VMEM((8, 24, T), F32),
            pltpu.SemaphoreType.DMA((HEADS,)),
            pltpu.SemaphoreType.DMA((HEADS,)),
            pltpu.SemaphoreType.DMA((26,)),
            pltpu.SemaphoreType.DMA((26,)),
            pltpu.SemaphoreType.DMA,
            pltpu.SemaphoreType.DMA,
        ],
        compiler_params=pltpu.CompilerParams(
            collective_id=0, has_side_effects=True, vmem_limit_bytes=62 * 2**20
        ),
        cost_estimate=pl.CostEstimate(flops=20 * 10**9, bytes_accessed=2 * 10**6, transcendentals=0),
        name="mixer",
    )(
        queries, keys, values, out_gate, write_rate.T, decay.T, head_gain[None, :],
        residual, out_proj, ffn_gain[None, :], listed,
    )


PEERS = 32
ROWS = 16
HALF = T // 2
GROUP = PEERS * ROWS
AG_CHUNKS = (
    ((1, 0), (1, 1), (2, 0), (2, 1), (3, 0), (3, 1), (4, 0)),
    ((1, 1), (1, 0), (2, 1), (2, 0), (3, 1), (3, 0), (4, 1)),
)
WIDE = D // 2
RS_CHUNKS = (
    ((4, 1), (3, 0), (3, 1), (2, 0), (2, 1), (1, 0), (1, 1)),
    ((4, 0), (3, 1), (3, 0), (2, 1), (2, 0), (1, 1), (1, 0)),
)
BEHIND = {1: 1, 2: 3, 3: 5, 4: 7}
AHEAD = {1: 2, 2: 4, 3: 6, 4: 7}
OFFSETS = (0, -1, 1, -2, 2, -3, 3, 4)


def moe_kernel(
    x_ref, info_ref, wg_hbm, wu_hbm, wd_hbm, out_ref,
    act_ref, xg, stage, rows, outb, ret, rs_out, rs_in, y_ref, pick, high, low, wg, wu, wd,
    w_sem, ag_send, ag_recv, in_send, in_recv, back_send, back_recv, rs_send, rs_recv,
):
    ctx = lax.axis_index("ctx")
    exp = lax.axis_index("exp")
    yy, zz = exp // 8, exp % 8
    mine = ctx * 4 + yy
    barrier = pltpu.get_barrier_semaphore()

    def peer(k):
        c, y = (ctx + k // 4) % 8, (yy + k % 4) % 4
        return c * 4 + y, {"ctx": c, "exp": y * 8 + zz}

    def along(step):
        return {"ctx": ctx, "exp": yy * 8 + (zz + step + 8) % 8}

    weights = [
        pltpu.make_async_copy(s, d, w_sem.at[i])
        for i, (s, d) in enumerate(((wg_hbm, wg), (wu_hbm, wu), (wd_hbm, wd)))
    ]
    for copy in weights:
        copy.start()

    def greet(k, carry):
        pl.semaphore_signal(barrier, inc=1, device_id=peer(k)[1], device_id_type=MESH)
        return carry

    for step in (1, -1):
        pl.semaphore_signal(barrier, inc=1, device_id=along(step), device_id_type=MESH)
    lax.fori_loop(1, PEERS, greet, 0)
    xg[0] = x_ref[...]
    pl.semaphore_wait(barrier, PEERS + 1)

    def half(h):
        return pl.ds(h * HALF, HALF)

    def wide(c):
        return pl.ds(c * WIDE, WIDE)

    def gather(way, i):
        d, h = AG_CHUNKS[way][i % 7]
        slot = (BEHIND, AHEAD)[way]
        cols = wide(i // 7)
        src = x_ref.at[half(h), cols] if d == 1 else xg.at[slot[d - 1], half(h), cols]
        return pltpu.make_async_remote_copy(
            src_ref=src,
            dst_ref=xg.at[slot[d], half(h), cols],
            send_sem=ag_send.at[way, i],
            recv_sem=ag_recv.at[way, i],
            device_id=along((1, -1)[way]),
            device_id_type=MESH,
        )

    def pass_on(first, end):
        for i in range(first, end):
            for way in (0, 1):
                gather(way, i).wait_recv()
                if i + 2 < 14:
                    gather(way, i + 2).start()

    for i in (0, 1):
        for way in (0, 1):
            gather(way, i).start()

    row = lax.broadcasted_iota(jnp.int32, (GROUP, T), 0)
    slot_of = (row % CAP).astype(F32)
    spread = (
        lax.broadcasted_iota(jnp.int32, (GROUP, PEERS), 0) // ROWS
        == lax.broadcasted_iota(jnp.int32, (GROUP, PEERS), 1)
    )
    spread_b, spread_f = spread.astype(F32).astype(BF16), spread.astype(F32)
    earlier = (
        lax.broadcasted_iota(jnp.int32, (T, T), 0) < lax.broadcasted_iota(jnp.int32, (T, T), 1)
    ).astype(F32).astype(BF16)
    named = (lax.broadcasted_iota(jnp.int32, (PEERS, T), 0) * 8 + zz).astype(F32)

    def tables(g, *sources):
        for s in sources:
            info = info_ref[(zz + OFFSETS[g * 4 + s] + 8) % 8]
            member = jnp.zeros((PEERS, T), F32)
            weight = jnp.zeros((PEERS, T), F32)
            for j in range(TOP):
                hit = info[j : j + 1] == named
                member = member + jnp.where(hit, 1.0, 0.0)
                weight = weight + jnp.where(hit, info[TOP + j : TOP + j + 1], 0.0)
            member_b = member.astype(BF16)
            before = jnp.dot(member_b, earlier, preferred_element_type=F32)
            here = jnp.dot(spread_b, member_b, preferred_element_type=F32)
            place = jnp.dot(spread_b, before.astype(BF16), preferred_element_type=F32)
            share = jnp.dot(spread_f, weight, precision=HIGHEST, preferred_element_type=F32)
            taken = (here > 0.5) & (place == slot_of) & (row // CAP % 4 == s)
            at = pl.ds(s * T, T)
            pick[g, :, at] = jnp.where(taken, 1.0, 0.0).astype(BF16)
            scaled = jnp.where(taken, share, 0.0).T
            top = scaled.astype(BF16)
            high[g, at, :] = top
            low[g, at, :] = (scaled - top.astype(F32)).astype(BF16)

    def tiles(body, first=0, end=D // 512):
        def run(i, carry):
            body(pl.ds(pl.multiple_of(i * 512, 512), 512))
            return carry

        lax.fori_loop(first, end, run, 0)

    def own(p):
        return pl.ds(pl.multiple_of(p * ROWS, ROWS), ROWS)

    def exchange(src, dst, send, recv, g, cols):
        def go(k, carry):
            p, device = peer(k)
            pltpu.make_async_remote_copy(
                src_ref=src.at[g, own(p), cols],
                dst_ref=dst.at[g, own(mine), cols],
                send_sem=send,
                recv_sem=recv,
                device_id=device,
                device_id_type=MESH,
            ).start()
            return carry

        lax.fori_loop(1, PEERS, go, 0)
        dst[g, own(mine), cols] = src[g, own(mine), cols]

    def all_of(ref, sem, g, cols):
        some = ref.at[g, pl.ds(0, GROUP - ROWS), cols]
        return pltpu.make_async_copy(some, some, sem)

    def dispatch(g, c):
        def tile(at):
            x = xg[g * 4 : g * 4 + 4, :, at].reshape(GROUP, 512)
            stage[g, :, at] = jnp.dot(pick[g], x, preferred_element_type=F32).astype(BF16)

        tiles(tile, 2 * c, 2 * c + 2)
        exchange(stage, rows, in_send.at[g, c], in_recv.at[g, c], g, wide(c))

    def experts(g):
        for c in (0, 1):
            all_of(rows, in_recv.at[g, c], g, wide(c)).wait()

        def tile(i, carry):
            at = pl.ds(pl.multiple_of(i * 256, 256), 256)
            x = rows[g, at, :]
            gate = jnp.dot(x, wg[...], preferred_element_type=F32)
            up = jnp.dot(x, wu[...], preferred_element_type=F32)
            act_ref[at, :] = (gate / (1.0 + jnp.exp(-gate)) * up).astype(BF16)
            return carry

        lax.fori_loop(0, GROUP // 256, tile, 0)
        for c in (0, 1):
            def down(at):
                outb[g, :, at] = jnp.dot(
                    act_ref[...], wd[:, at], preferred_element_type=F32
                ).astype(BF16)

            tiles(down, 2 * c, 2 * c + 2)
            exchange(outb, ret, back_send.at[g, c], back_recv.at[g, c], g, wide(c))

    def combine(g, c):
        all_of(ret, back_recv.at[g, c], g, wide(c)).wait()

        def tile(at):
            r = ret[g, :, at]
            total = jnp.dot(high[g], r, preferred_element_type=F32) + jnp.dot(
                low[g], r, preferred_element_type=F32
            )
            y_ref[g * 4 : g * 4 + 4, :, at] = total.reshape(4, T, 512)

        tiles(tile, 2 * c, 2 * c + 2)

    tables(0, 0, 1)
    pass_on(0, 1)
    tables(0, 2)
    pass_on(1, 2)
    tables(0, 3)
    pass_on(2, 4)
    dispatch(0, 0)
    pass_on(4, 5)
    tables(1, 0, 1)
    pass_on(5, 6)
    tables(1, 2, 3)
    pass_on(6, 7)
    dispatch(1, 0)
    pass_on(7, 11)
    dispatch(0, 1)
    pass_on(11, 14)
    dispatch(1, 1)
    for copy in weights:
        copy.wait()
    experts(0)
    experts(1)

    def reduce(c, way, i):
        return pltpu.make_async_remote_copy(
            src_ref=rs_out.at[way, i, :, wide(c)],
            dst_ref=rs_in.at[way, i, :, wide(c)],
            send_sem=rs_send.at[c, way, i],
            recv_sem=rs_recv.at[c, way, i],
            device_id=along((1, -1)[way]),
            device_id_type=MESH,
        )

    def reduce_step(c, i):
        for way in (0, 1):
            d, h = RS_CHUNKS[way][i]
            part = y_ref[(AHEAD, BEHIND)[way][d], half(h), wide(c)]
            if i >= 2:
                reduce(c, way, i - 2).wait_recv()
                part = part + rs_in[way, i - 2, :, wide(c)].astype(F32)
            rs_out[way, i, :, wide(c)] = part.astype(BF16)
            reduce(c, way, i).start()

    combine(1, 0)
    reduce_step(0, 0)
    reduce_step(0, 1)
    combine(0, 0)
    for i in range(2, 5):
        reduce_step(0, i)
    combine(1, 1)
    reduce_step(1, 0)
    reduce_step(0, 5)
    reduce_step(1, 1)
    reduce_step(0, 6)
    combine(0, 1)
    for i in range(2, 7):
        reduce_step(1, i)
    for c in (0, 1):
        for i in (5, 6):
            for way in (0, 1):
                reduce(c, way, i).wait_recv()
        for h in (0, 1):
            total = y_ref[0, half(h), wide(c)]
            for way in (0, 1):
                total = total + rs_in[way, RS_CHUNKS[way].index((1, h)), :, wide(c)].astype(F32)
            out_ref[half(h), wide(c)] = total

    for i in range(7):
        for way in (0, 1):
            for c in (0, 1):
                gather(way, i + 7 * c).wait_send()
                reduce(c, way, i).wait_send()
    for g in (0, 1):
        for c in (0, 1):
            all_of(stage, in_send.at[g, c], g, wide(c)).wait()
            all_of(outb, back_send.at[g, c], g, wide(c)).wait()


def moe(x, info, w_gate, w_up, w_down):
    group = pltpu.VMEM((2, GROUP, D), BF16)
    table = pltpu.VMEM((2, GROUP, GROUP), BF16)
    ring = pltpu.VMEM((2, 7, HALF, D), BF16)
    dma = pltpu.SemaphoreType.DMA
    vmem, anywhere = pl.BlockSpec(memory_space=pltpu.VMEM), pl.BlockSpec(memory_space=pl.ANY)
    return pl.pallas_call(
        moe_kernel,
        out_shape=jax.ShapeDtypeStruct((T, D), F32),
        in_specs=[vmem, vmem, anywhere, anywhere, anywhere],
        out_specs=vmem,
        scratch_shapes=[
            pltpu.VMEM((GROUP, 512), BF16),
            pltpu.VMEM((8, T, D), BF16),
            group, group, group, group, ring, ring,
            pltpu.VMEM((8, T, D), F32),
            table, table, table,
            pltpu.VMEM((D, 512), BF16), pltpu.VMEM((D, 512), BF16), pltpu.VMEM((512, D), BF16),
            dma((3,)), dma((2, 14)), dma((2, 14)), dma((2, 2)), dma((2, 2)), dma((2, 2)), dma((2, 2)),
            dma((2, 2, 7)), dma((2, 2, 7)),
        ],
        compiler_params=pltpu.CompilerParams(
            collective_id=1, has_side_effects=True, vmem_limit_bytes=62 * 2**20
        ),
        cost_estimate=pl.CostEstimate(flops=12 * 10**9, bytes_accessed=10**7, transcendentals=0),
        name="moe",
    )(x, info, w_gate, w_up, w_down)


def local(
    queries, keys, values, out_gate, write_rate, decay, head_gain, residual, out_proj, ffn_gain,
    expert_ids, route_weight, w_gate, w_up, w_down, ablate_mask, direction,
):
    listed = jnp.concatenate(
        [expert_ids[0].T.astype(F32), route_weight[0].T, jnp.zeros((4, T), F32)], axis=0
    )
    hidden_sum, ffn_in, info = mixer(
        queries[0], keys[0], values[0], out_gate[0], write_rate[0], decay[0], head_gain, residual[0],
        out_proj, ffn_gain, listed,
    )
    moe_sum = moe(ffn_in, info, w_gate[0], w_up[0], w_down[0])
    combined = hidden_sum + moe_sum
    unit_dir = direction / jnp.sqrt(jnp.sum(direction * direction) + 1e-06)
    along = jnp.sum(combined * unit_dir[None, :], axis=1)
    mask_f = ablate_mask[0].astype(F32)
    layer_out = combined - (mask_f * along)[:, None] * unit_dir[None, :]
    return layer_out.astype(BF16)[None]


def solution(mesh):
    tokens = P("exp", "ctx", None)
    experts = P(("ctx", "exp"), None, None)
    placed = (
        tokens, tokens, tokens, tokens, tokens, tokens, P(), tokens, P("ctx", None), P(),
        tokens, tokens, experts, experts, experts, P("exp", "ctx"), P(),
    )
    return jax.shard_map(local, mesh=mesh, in_specs=placed, out_specs=tokens, check_vma=False)
```
